32 devices in a mesh: group: 2 (over y), head: 8 (over z, x), dp: 2 (over core).
Axes of the slice: x: 2, y: 2, z: 4, core: 2. Of those that a mesh axis runs over, the one named last changes fastest.
Arguments:
- queries: bfloat16 [32, 16384], P(('group', 'dp'), 'head'), parts along dimension 0, may hold values from -6 to 6
- new_kv: bfloat16 [32, 2, 1024], P(('group', 'dp')), parts along dimension 0, may hold values from -6 to 6
- positions: int32 [32], P(('group', 'dp')), parts along dimension 0, may hold values from 256 to 1023
- lengths: int32 [32], P(('group', 'dp')), parts along dimension 0, may hold values from 2 to 256, as said below
- kv_codes: bfloat16 [32, 2, 256, 1024], P(('group', 'dp'), None, 'head'), parts along dimension 0, may hold values from -8 to 7, as said below
- kv_scales: float32 [32, 2, 8, 256], P(('group', 'dp'), None, None, 'head'), parts along dimension 0, may hold values from 0.1 to 40
- wo_codes: bfloat16 [16384, 16384], P('head'), may hold values from -8 to 7, as said below
- wo_scales: float32 [16384], P('head'), may hold values from 0.004 to 0.03
- residual: bfloat16 [32, 16384], P(('group', 'dp'), 'head'), parts along dimension 0, may hold values from -6 to 6
Outputs:
- hidden_out: bfloat16 [32, 16384], P(('group', 'dp'), 'head'), parts along dimension 0
The draws below stay inside these ranges and needn't reach their ends.
There are 2 independent parts, one for each index of `group`. The reference program is written for one: setup_inputs(seed, part) draws one part's arguments, and reference() takes and returns one part's arrays. A program takes and returns all parts, laid end to end along the dimension named above; an argument that names none is the same for every part. Nothing has to cross between parts.
Inputs may be any that keep to these rules, and one draw needn't show every extreme that they name: Each row has at least two live slots, which are slots 0 to lengths - 1 of every key-value head; some row is full (256 live slots). `kv_codes`: integer codes. `wo_codes`: integer codes.
All inputs are finite; a program needn't handle non-finite values.
Results may differ from the reference program's by a relative error of at most 0.0089.
Values may be sent and summed in bfloat16 or wider, within the bound.
No kernel may reach another device: no remote copies, remote signals or barrier semaphores. Data moves between devices by JAX's collectives and lax.ppermute only.
A program may use at most 128 MiB of HBM per device.

```python
import math
import jax
import jax.numpy as jnp
from jax import lax

D = 16384
H = 128
KVH = 8
HD = 128
CTX = 256
ROWS = 16


def draw_lengths(key, part):
    key_base, key_extra = jax.random.split(jax.random.fold_in(key, 11))
    drawn = jax.random.randint(key_base, (ROWS,), 2, CTX + 1)
    full_row = jax.random.randint(key_extra, (), 0, ROWS)
    return jnp.where(jnp.arange(ROWS) == full_row, CTX, drawn).astype(jnp.int32)


def draw_kv_codes(key, part):
    drawn = jax.random.randint(jax.random.fold_in(key, 3), (ROWS, 2, CTX, KVH, HD), -8, 8).astype(jnp.float32)
    return drawn.reshape(ROWS, 2, CTX, KVH * HD).astype(jnp.bfloat16)


def draw_kv_scales(key, part):
    key_base = jax.random.fold_in(jax.random.fold_in(key, 5), 0)
    drawn = jnp.exp(jax.random.uniform(key_base, (ROWS, 2, KVH, CTX), minval=math.log(0.1), maxval=math.log(0.3)))
    return drawn.astype(jnp.float32)


def draw_wo_codes(key, part):
    drawn = jax.random.randint(jax.random.fold_in(key, 7), (H * HD, D), -8, 8).astype(jnp.float32)
    return drawn.astype(jnp.bfloat16)


def place_ends(result, stream_key, low, top_value):
    longest = result.shape.index(max(result.shape))
    spots = []
    for shift in (0, 1):
        where = [jax.random.randint(jax.random.fold_in(stream_key, axis), (), 0, length) for axis, length in enumerate(result.shape)]
        where[longest] = (where[longest] + shift) % result.shape[longest]
        spots.append(tuple(where))
    return result.at[spots[0]].set(low).at[spots[1]].set(top_value)


def block_scale(key, shape, pieces, smallest, high):
    loudness = 1.0
    for dim, parts in pieces:
        draws = jax.random.uniform(jax.random.fold_in(jax.random.fold_in(key, 6), dim), (parts,), jnp.float32, smallest / len(pieces), high / len(pieces))
        loudness = loudness * jnp.repeat(jnp.exp(draws), shape[dim] // parts).reshape((-1,) + (1,) * (len(shape) - 1 - dim))
    return loudness


def bell_draw(own_key, extent, deviation, bound, cuts=(), kind=jnp.bfloat16):
    values = deviation * jax.random.normal(own_key, extent, jnp.float32)
    if cuts:
        values = values * block_scale(own_key, extent, cuts, -0.22, 0.18)
    return jnp.clip(values, -bound, bound).astype(kind)


def setup_inputs(seed: int = 0, part: int = 0) -> dict:
    key_of = jax.random.split(jax.random.key(seed), 10)
    part_keys = jax.random.split(jax.random.fold_in(key_of[9], part), 10)
    queries = bell_draw(part_keys[0], (ROWS, H * HD), 1.0, 6.0, ((0, 2), (1, 8)))
    new_kv = bell_draw(part_keys[1], (ROWS, 2, KVH * HD), 1.0, 6.0, ((0, 2),))
    positions = place_ends(jax.random.randint(part_keys[2], (ROWS,), CTX, 4 * CTX), jax.random.fold_in(part_keys[2], 1), CTX, (4 * CTX) - 1).astype(jnp.int32)
    lengths = draw_lengths(jax.random.fold_in(jax.random.fold_in(key_of[9], part), 71), part)
    kv_codes = draw_kv_codes(jax.random.fold_in(jax.random.fold_in(key_of[9], part), 71), part)
    kv_scales = draw_kv_scales(jax.random.fold_in(jax.random.fold_in(key_of[9], part), 71), part)
    wo_codes = draw_wo_codes(jax.random.fold_in(key_of[9], 71), part)
    wo_scales = jnp.clip(jnp.exp(math.log(0.03) - 2.014903 * jax.random.uniform(key_of[7], (D,), jnp.float32) ** block_scale(key_of[7], (D,), ((0, 8),), -0.2, 0.2)), 0.004, 0.03)
    residual = bell_draw(part_keys[8], (ROWS, D), 1.0, 6.0, ((0, 2), (1, 8)))
    return {"queries": queries, "new_kv": new_kv, "positions": positions, "lengths": lengths, "kv_codes": kv_codes, "kv_scales": kv_scales, "wo_codes": wo_codes, "wo_scales": wo_scales, "residual": residual}


ROPE_BASE = 500000.0
NEG_FILL = -1.0e30


def rotary(values_in, positions):
    half_dim = values_in.shape[-1] // 2
    inverse_rate = ROPE_BASE ** (-(jnp.arange(half_dim, dtype=jnp.float32) * (2.0 / values_in.shape[-1])))
    angles = positions.astype(jnp.float32)[:, None, None] * inverse_rate
    cosine = jnp.cos(angles)
    sine_part = jnp.sin(angles)
    lower_half = values_in[..., :half_dim]
    upper_half = values_in[..., half_dim:]
    return jnp.concatenate([lower_half * cosine - upper_half * sine_part, upper_half * cosine + lower_half * sine_part], axis=-1)


def hadamard(size_needed):
    index_row = jnp.arange(size_needed, dtype=jnp.int32)
    common = jnp.bitwise_and(index_row[:, None], index_row[None, :])
    parity = jnp.zeros_like(common)
    for bit_pos in range(max(size_needed.bit_length() - 1, 0)):
        parity = parity + jnp.right_shift(common, bit_pos) % 2
    return jnp.where(parity % 2 == 0, 1.0, -1.0).astype(jnp.float32)


def reference(queries, new_kv, positions, lengths, kv_codes, kv_scales, wo_codes, wo_scales, residual):
    n_rows = queries.shape[0]
    group_size = H // KVH
    score_scale = HD ** -0.5
    query_rot = rotary(queries.reshape(n_rows, H, HD).astype(jnp.float32), positions).astype(jnp.bfloat16)
    fresh_keys = rotary(new_kv[:, 0].reshape(n_rows, KVH, HD).astype(jnp.float32), positions).astype(jnp.bfloat16)
    fresh_values = new_kv[:, 1].reshape(n_rows, KVH, HD).astype(jnp.float32)
    query_groups = query_rot.reshape(n_rows, KVH, group_size, HD).astype(jnp.float32)
    cache_codes = kv_codes.reshape(n_rows, 2, CTX, KVH, HD).astype(jnp.float32)
    cache_scales = kv_scales
    raw_scores = jnp.einsum("rgjd,rtgd->rgjt", query_groups, cache_codes[:, 0], precision=lax.Precision.HIGHEST)
    scores = raw_scores * cache_scales[:, 0][:, :, None, :] * score_scale
    is_valid = (jnp.arange(CTX, dtype=jnp.int32)[None, :] < lengths[:, None])[:, None, None, :]
    scores = jnp.where(is_valid, scores, NEG_FILL)
    fresh_score = jnp.einsum("rgjd,rgd->rgj", query_groups, fresh_keys.astype(jnp.float32), precision=lax.Precision.HIGHEST) * score_scale
    peak_all = jnp.maximum(jnp.max(scores, axis=-1), fresh_score)
    weights = jnp.where(is_valid, jnp.exp(scores - peak_all[..., None]), 0.0)
    fresh_weight = jnp.exp(fresh_score - peak_all)
    total_all = jnp.sum(weights, axis=-1) + fresh_weight
    weighted = jnp.einsum("rgjt,rtgd->rgjd", weights * cache_scales[:, 1][:, :, None, :], cache_codes[:, 1], precision=lax.Precision.HIGHEST)
    weighted = weighted + fresh_weight[..., None] * fresh_values[:, :, None, :]
    attended = (weighted / total_all[..., None]).reshape(n_rows, H, HD).astype(jnp.bfloat16)
    sylvester = hadamard(H)
    rotated = jnp.einsum("ij,rjd->rid", sylvester, attended.astype(jnp.float32), precision=lax.Precision.HIGHEST) * (H ** -0.5)
    flat_rows = rotated.reshape(n_rows, H * HD).astype(jnp.bfloat16)
    projected = jnp.dot(flat_rows, wo_codes, preferred_element_type=jnp.float32) * wo_scales
    return (residual.astype(jnp.float32) + projected).astype(jnp.bfloat16)
```

```python
import functools
import jax
import jax.numpy as jnp
from jax import lax
from jax.experimental import pallas as pl
from jax.experimental.pallas import tpu as pltpu
from jax.sharding import PartitionSpec as P

HD = 128
ROPE_BASE = 500000.0
NEG_FILL = -1e30
STAT_ROWS = 16
MIB = 1 << 20
VMEM = pltpu.MemorySpace.VMEM
SMEM = pltpu.MemorySpace.SMEM


def split3(value):
    high = value.astype(jnp.bfloat16)
    rest = value - high.astype(jnp.float32)
    middle = rest.astype(jnp.bfloat16)
    low = (rest - middle.astype(jnp.float32)).astype(jnp.bfloat16)
    return high, middle, low


def contract(left, right, dims):
    return lax.dot_general(left, right, (dims, ((), ())), preferred_element_type=jnp.float32)


def rotary_tables(positions):
    half_dim = HD // 2
    inverse_rate = ROPE_BASE ** (-(jnp.arange(half_dim, dtype=jnp.float32) * (2.0 / HD)))
    angles = positions.astype(jnp.float32)[:, None] * inverse_rate
    cosine = jnp.cos(angles)
    sine = jnp.sin(angles)
    return jnp.concatenate([cosine, cosine], -1), jnp.concatenate([-sine, sine], -1)


def attend(scalars, gathered, cosine, sine, new_kv, kv_codes, key_scales, value_scales):
    n_src, n_rows, width = gathered.shape
    heads_here = width // HD
    n_heads = n_src * heads_here
    block_len = kv_codes.shape[2]
    n_kv = kv_codes.shape[3] // HD
    group = n_heads // n_kv
    score_scale = HD ** (-0.5)

    def body(s_ref, q_ref, cos_ref, sin_ref, new_ref, kv_ref, ks_ref, vs_ref, out_ref, qs, ks):
        cos, sin = cos_ref[...], sin_ref[...]

        def rotate(tile):
            return tile * cos + pltpu.roll(tile, HD // 2, 1) * sin

        for src in range(n_src):
            block = q_ref[src].astype(jnp.float32)
            for j in range(heads_here):
                head = src * heads_here + j
                qs[n_rows * head : n_rows * (head + 1), :] = rotate(block[:, HD * j : HD * (j + 1)])
        fresh = new_ref[:, 0, :].astype(jnp.float32)
        for k in range(n_kv):
            ks[n_rows * k : n_rows * (k + 1), :] = rotate(fresh[:, HD * k : HD * (k + 1)])

        first_slot = s_ref[n_rows]
        is_first = first_slot == 0
        lane_group = lax.broadcasted_iota(jnp.int32, (1, n_heads), 1) // group
        slot = first_slot + lax.broadcasted_iota(jnp.int32, (block_len, n_heads), 0)
        own_kv = lax.broadcasted_iota(jnp.int32, (n_kv, n_heads), 0) == lane_group
        for r in range(n_rows):
            query = qs[pl.ds(r, n_heads, stride=n_rows), :].astype(jnp.bfloat16)
            keys = jnp.concatenate(
                [kv_ref[r, 0, :, HD * k : HD * (k + 1)] for k in range(n_kv)], axis=0
            )
            values = jnp.concatenate(
                [kv_ref[r, 1, :, HD * k : HD * (k + 1)] for k in range(n_kv)], axis=0
            )
            raw = contract(keys, query, ((1,), (1,)))
            raw_own = jnp.zeros((block_len, n_heads), jnp.float32)
            for k in range(n_kv):
                raw_own = jnp.where(lane_group == k, raw[block_len * k : block_len * (k + 1)], raw_own)
            is_valid = slot < s_ref[r]
            scores = jnp.where(is_valid, raw_own * ks_ref[r] * score_scale, NEG_FILL)
            fresh_key = ks[pl.ds(r, n_kv, stride=n_rows), :].astype(jnp.bfloat16)
            fresh_raw = contract(fresh_key, query, ((1,), (1,)))
            fresh_score = jnp.sum(jnp.where(own_kv, fresh_raw, 0.0), axis=0, keepdims=True) * score_scale
            fresh_score = jnp.where(is_first, fresh_score, NEG_FILL)
            peak = jnp.maximum(jnp.max(scores, axis=0, keepdims=True), fresh_score)
            weights = jnp.where(is_valid, jnp.exp(scores - peak), 0.0)
            fresh_weight = jnp.where(is_first, jnp.exp(fresh_score - peak), 0.0)
            total = jnp.sum(weights, axis=0, keepdims=True) + fresh_weight
            scaled = weights * vs_ref[r]
            spread = jnp.concatenate(
                [jnp.where(lane_group == k, scaled, 0.0) for k in range(n_kv)], axis=0
            )
            high = spread.astype(jnp.bfloat16)
            low = (spread - high.astype(jnp.float32)).astype(jnp.bfloat16)
            fresh_spread = jnp.where(own_kv, fresh_weight, 0.0)
            fresh_high = fresh_spread.astype(jnp.bfloat16)
            fresh_low = (fresh_spread - fresh_high.astype(jnp.float32)).astype(jnp.bfloat16)
            fresh_value = jnp.concatenate(
                [new_ref[r : r + 1, 1, HD * k : HD * (k + 1)] for k in range(n_kv)], axis=0
            )
            both = ((0,), (0,))
            summed = contract(high, values, both) + contract(low, values, both)
            summed = summed + (
                contract(fresh_high, fresh_value, both) + contract(fresh_low, fresh_value, both)
            )
            out_ref[r, 0:n_heads, :] = summed.astype(jnp.bfloat16)
            parts = split3(peak) + split3(total)
            pad = jnp.zeros((STAT_ROWS - len(parts), n_heads), jnp.float32)
            stats = jnp.concatenate([part.astype(jnp.float32) for part in parts] + [pad], axis=0)
            out_ref[r, n_heads : n_heads + STAT_ROWS, :] = stats.astype(jnp.bfloat16)

    return pl.pallas_call(
        body,
        out_shape=jax.ShapeDtypeStruct((n_rows, n_heads + STAT_ROWS, HD), jnp.bfloat16),
        in_specs=[pl.BlockSpec(memory_space=SMEM)] + [pl.BlockSpec(memory_space=VMEM)] * 7,
        out_specs=pl.BlockSpec(memory_space=VMEM),
        scratch_shapes=[
            pltpu.VMEM((n_rows * n_heads, HD), jnp.float32),
            pltpu.VMEM((n_rows * n_kv, HD), jnp.float32),
        ],
        compiler_params=pltpu.CompilerParams(vmem_limit_bytes=12 * MIB),
        name="attend",
    )(scalars, gathered, cosine, sine, new_kv, kv_codes, key_scales, value_scales)


def settle(main, stats, n_heads, stat_row):
    n_src = main.shape[0]
    depth = main.shape[2]
    heads_root = n_heads ** (-0.5)

    def body(main_ref, stat_ref, out_ref):
        peaks, totals = [], []
        for b in range(n_src):
            part = stat_ref[b, stat_row : stat_row + STAT_ROWS, :].astype(jnp.float32)
            peaks.append(part[0:1] + part[1:2] + part[2:3])
            totals.append(part[3:4] + part[4:5] + part[5:6])
        peak = functools.reduce(jnp.maximum, peaks)
        scales = [jnp.exp(p - peak) for p in peaks]
        total = functools.reduce(jnp.add, [s * t for s, t in zip(scales, totals)])
        common = lax.broadcasted_iota(jnp.int32, (n_heads, n_heads), 0) & lax.broadcasted_iota(
            jnp.int32, (n_heads, n_heads), 1
        )
        bits = (n_heads - 1).bit_length()
        parity = common
        for bit in range(1, bits):
            parity = parity ^ (common >> bit)
        sign = jnp.where((parity & 1) == 0, heads_root, -heads_root)
        acc = jnp.zeros((n_heads, depth), jnp.float32)
        for b in range(n_src):
            mixed = sign * (scales[b] / total)
            high = mixed.astype(jnp.bfloat16)
            low = (mixed - high.astype(jnp.float32)).astype(jnp.bfloat16)
            value = main_ref[b, 0:n_heads, :]
            acc = acc + jnp.dot(high, value, preferred_element_type=jnp.float32)
            acc = acc + jnp.dot(low, value, preferred_element_type=jnp.float32)
        out_ref[...] = acc.astype(jnp.bfloat16)

    return pl.pallas_call(
        body,
        out_shape=jax.ShapeDtypeStruct((n_heads, depth), jnp.bfloat16),
        in_specs=[pl.BlockSpec(memory_space=VMEM)] * 2,
        out_specs=pl.BlockSpec(memory_space=VMEM),
        compiler_params=pltpu.CompilerParams(vmem_limit_bytes=16 * MIB),
        name="settle",
    )(main, stats)


def project(own_share, rows, wo, n_block, n_share):
    n_all, heads_here, _ = rows.shape
    depth = wo.shape[0]
    block_cols = wo.shape[1] // n_block
    piece = block_cols // n_share
    n_rows = n_all // n_share

    def body(own_ref, x_ref, wo_ref, out_ref, weights, wide, packed, sem):
        start = own_ref[0] * piece

        def fetch(b):
            cols = pl.ds(pl.multiple_of(b * block_cols + start, 128), piece)
            return pltpu.make_async_copy(wo_ref.at[:, cols], weights.at[b], sem.at[b])

        for b in range(n_block):
            fetch(b).start()
        wide[...] = x_ref[...].astype(jnp.float32).reshape(n_all * heads_here, HD)
        for j in range(heads_here):
            pieces = [
                wide[pl.ds(s * heads_here + j, n_rows, stride=heads_here * n_share), :]
                for s in range(n_share)
            ]
            packed[:, HD * j : HD * (j + 1)] = jnp.concatenate(pieces, axis=0).astype(jnp.bfloat16)
        x = packed[...]
        for b in range(n_block):
            fetch(b).wait()
            share = jnp.dot(x, weights[b], preferred_element_type=jnp.float32)
            for s in range(n_share):
                out_ref[b * n_share + s] = share[s * n_rows : (s + 1) * n_rows].astype(jnp.bfloat16)

    return pl.pallas_call(
        body,
        out_shape=jax.ShapeDtypeStruct((n_block * n_share, n_rows, piece), jnp.bfloat16),
        in_specs=[
            pl.BlockSpec(memory_space=SMEM),
            pl.BlockSpec(memory_space=VMEM),
            pl.BlockSpec(memory_space=pl.ANY),
        ],
        out_specs=pl.BlockSpec(memory_space=VMEM),
        scratch_shapes=[
            pltpu.VMEM((n_block, depth, piece), wo.dtype),
            pltpu.VMEM((n_all * heads_here, HD), jnp.float32),
            pltpu.VMEM((n_all, heads_here * HD), jnp.bfloat16),
            pltpu.SemaphoreType.DMA((n_block,)),
        ],
        compiler_params=pltpu.CompilerParams(vmem_limit_bytes=44 * MIB),
        name="project",
    )(own_share, rows, wo)


def finish(shares, scales, residual, n_share):
    n_all, n_rows, piece = shares.shape

    def body(share_ref, scale_ref, res_ref, out_ref):
        for s in range(n_share):
            total = share_ref[s].astype(jnp.float32)
            for h in range(1, n_all // n_share):
                total = total + share_ref[h * n_share + s].astype(jnp.float32)
            cols = slice(s * piece, (s + 1) * piece)
            out_ref[:, cols] = (
                res_ref[:, cols].astype(jnp.float32) + total * scale_ref[:, cols]
            ).astype(jnp.bfloat16)

    return pl.pallas_call(
        body,
        out_shape=jax.ShapeDtypeStruct(residual.shape, jnp.bfloat16),
        in_specs=[pl.BlockSpec(memory_space=VMEM)] * 3,
        out_specs=pl.BlockSpec(memory_space=VMEM),
        compiler_params=pltpu.CompilerParams(vmem_limit_bytes=16 * MIB),
        name="finish",
    )(shares, scales, residual)


def exchange(block, axes):
    return lax.all_to_all(block, axes, split_axis=0, concat_axis=0, tiled=True)


def on_device(
    queries, new_kv, positions, lengths, kv_codes, kv_scales, wo_codes, wo_scales, residual
):
    n_head = lax.axis_size("head")
    n_share = lax.axis_size("dp")
    my_head = lax.axis_index("head")
    my_share = lax.axis_index("dp")
    n_rows, width = queries.shape
    heads_here = width // HD
    n_heads = heads_here * n_head
    n_kv = new_kv.shape[2] // HD
    block_len = kv_codes.shape[2]
    own_cols = wo_codes.shape[1] // n_head

    gathered = exchange(jnp.broadcast_to(queries, (n_head, n_rows, width)), "head")
    cosine, sine = rotary_tables(positions)
    spread = jnp.repeat(jnp.swapaxes(kv_scales, 2, 3), n_heads // n_kv, axis=3)
    scalars = jnp.concatenate([lengths, (my_head * block_len).reshape(1)]).astype(jnp.int32)
    partial = attend(
        scalars, gathered, cosine, sine, new_kv, kv_codes, spread[:, 0], spread[:, 1]
    )

    cuts = max(1, n_head // n_rows)
    depth = HD // cuts
    if cuts == 1:
        main = exchange(partial, "head")
        rotated = settle(main, main, n_heads, n_heads)
    else:
        values = partial[:, :n_heads].reshape(n_rows, n_heads, cuts, depth).swapaxes(1, 2)
        stats = partial[:, n_heads:].reshape(n_rows, 1, STAT_ROWS * cuts, depth)
        stats = jnp.broadcast_to(stats, (n_rows, cuts) + stats.shape[2:])
        message = jnp.concatenate([values, stats], axis=2)
        received = exchange(message.reshape((n_head,) + message.shape[2:]), "head")
        rotated = settle(
            received[:, :n_heads], received[:, n_heads:].reshape(n_head, STAT_ROWS, HD), n_heads, 0
        )
    copies = jnp.broadcast_to(
        rotated.reshape(n_head, 1, heads_here, depth), (n_head, n_share, heads_here, depth)
    )
    rows = exchange(copies.reshape(n_head * n_share, heads_here, depth), ("head", "dp"))
    if cuts > 1:
        rows = rows.reshape(n_rows, cuts, n_share, heads_here, depth).transpose(0, 2, 3, 1, 4)
        rows = rows.reshape(n_rows * n_share, heads_here, HD)
    shares = exchange(
        project(my_share.reshape(1).astype(jnp.int32), rows, wo_codes, n_head, n_share), ("head", "dp"))
    return finish(shares, wo_scales.reshape(1, own_cols), residual, n_share)


def solution(mesh):
    placed = (
        P(("group", "dp"), "head"),
        P(("group", "dp"), None, None),
        P(("group", "dp")),
        P(("group", "dp")),
        P(("group", "dp"), None, "head", None),
        P(("group", "dp"), None, None, "head"),
        P("head", None),
        P("head"),
        P(("group", "dp"), "head"),
    )
    return jax.shard_map(
        on_device, mesh=mesh, in_specs=placed, out_specs=P(("group", "dp"), "head"), check_vma=False
    )
```

```python
import functools
import jax
import jax.numpy as jnp
from jax import lax
from jax.experimental import pallas as pl
from jax.experimental.pallas import tpu as pltpu
from jax.sharding import PartitionSpec as P

HD = 128
ROPE_BASE = 500000.0
NEG_FILL = -1e30
STAT_ROWS = 8
MIB = 1 << 20
VMEM = pltpu.MemorySpace.VMEM
SMEM = pltpu.MemorySpace.SMEM
HBM = pltpu.MemorySpace.HBM


def split3(value):
    high = value.astype(jnp.bfloat16)
    rest = value - high.astype(jnp.float32)
    middle = rest.astype(jnp.bfloat16)
    low = (rest - middle.astype(jnp.float32)).astype(jnp.bfloat16)
    return high, middle, low


def contract(left, right, dims):
    return lax.dot_general(left, right, (dims, ((), ())), preferred_element_type=jnp.float32)


def rotary_tables(positions):
    half_dim = HD // 2
    inverse_rate = ROPE_BASE ** (-(jnp.arange(half_dim, dtype=jnp.float32) * (2.0 / HD)))
    angles = positions.astype(jnp.float32)[:, None] * inverse_rate
    cosine = jnp.cos(angles)
    sine = jnp.sin(angles)
    return jnp.concatenate([cosine, cosine], -1), jnp.concatenate([-sine, sine], -1)


def weight_fetch(wo_ref, out_ref, sem, share, n_block, piece):
    def fetch(block, slot):
        start = block * (wo_ref.shape[1] // n_block) + share * piece
        cols = pl.ds(pl.multiple_of(start, 128), piece)
        return pltpu.make_async_copy(wo_ref.at[:, cols], out_ref.at[slot], sem.at[slot])

    return fetch


def attend(
    scalars, gathered, cosine, sine, new_kv, kv_codes, key_scales, value_scales, wo, n_early, piece
):
    n_src, n_rows, width = gathered.shape
    heads_here = width // HD
    n_heads = n_src * heads_here
    block_len = kv_codes.shape[2]
    n_kv = kv_codes.shape[3] // HD
    group = n_heads // n_kv
    score_scale = HD ** (-0.5)

    def body(
        s_ref, q_ref, cos_ref, sin_ref, new_hbm, kv_hbm, ks_ref, vs_ref, wo_ref, out_ref, early_ref,
        qs, ks, new_ref, kv_ref, new_sem, kv_sem, wo_sem,
    ):
        fetch_new = pltpu.make_async_copy(new_hbm, new_ref, new_sem)
        fetch_new.start()
        fetch_kv = [
            pltpu.make_async_copy(kv_hbm.at[r], kv_ref.at[r], kv_sem.at[r]) for r in range(n_rows)
        ]
        for copy in fetch_kv:
            copy.start()
        fetch = weight_fetch(wo_ref, early_ref, wo_sem, s_ref[n_rows + 1], n_src, piece)
        fetch_wo = [fetch(b, b) for b in range(n_early)]
        for copy in fetch_wo:
            copy.start()
        cos, sin = cos_ref[...], sin_ref[...]

        def rotate(tile):
            return tile * cos + pltpu.roll(tile, HD // 2, 1) * sin

        for src in range(n_src):
            block = q_ref[src].astype(jnp.float32)
            for j in range(heads_here):
                head = src * heads_here + j
                qs[n_rows * head : n_rows * (head + 1), :] = rotate(block[:, HD * j : HD * (j + 1)])
        fetch_new.wait()
        fresh = new_ref[:, 0, :].astype(jnp.float32)
        for k in range(n_kv):
            ks[n_rows * k : n_rows * (k + 1), :] = rotate(fresh[:, HD * k : HD * (k + 1)])

        first_slot = s_ref[n_rows]
        is_first = first_slot == 0
        lane_group = lax.broadcasted_iota(jnp.int32, (1, n_heads), 1) // group
        slot = first_slot + lax.broadcasted_iota(jnp.int32, (block_len, n_heads), 0)
        own_kv = lax.broadcasted_iota(jnp.int32, (n_kv, n_heads), 0) == lane_group
        for r in range(n_rows):
            fetch_kv[r].wait()
            query = qs[pl.ds(r, n_heads, stride=n_rows), :].astype(jnp.bfloat16)
            keys = jnp.concatenate(
                [kv_ref[r, 0, :, HD * k : HD * (k + 1)] for k in range(n_kv)], axis=0
            )
            values = jnp.concatenate(
                [kv_ref[r, 1, :, HD * k : HD * (k + 1)] for k in range(n_kv)], axis=0
            )
            raw = contract(keys, query, ((1,), (1,)))
            raw_own = jnp.zeros((block_len, n_heads), jnp.float32)
            for k in range(n_kv):
                raw_own = jnp.where(lane_group == k, raw[block_len * k : block_len * (k + 1)], raw_own)
            is_valid = slot < s_ref[r]
            scores = jnp.where(is_valid, raw_own * ks_ref[r] * score_scale, NEG_FILL)
            fresh_key = ks[pl.ds(r, n_kv, stride=n_rows), :].astype(jnp.bfloat16)
            fresh_raw = contract(fresh_key, query, ((1,), (1,)))
            fresh_score = jnp.sum(jnp.where(own_kv, fresh_raw, 0.0), axis=0, keepdims=True) * score_scale
            fresh_score = jnp.where(is_first, fresh_score, NEG_FILL)
            peak = jnp.maximum(jnp.max(scores, axis=0, keepdims=True), fresh_score)
            weights = jnp.where(is_valid, jnp.exp(scores - peak), 0.0)
            fresh_weight = jnp.where(is_first, jnp.exp(fresh_score - peak), 0.0)
            total = jnp.sum(weights, axis=0, keepdims=True) + fresh_weight
            scaled = weights * vs_ref[r]
            spread = jnp.concatenate(
                [jnp.where(lane_group == k, scaled, 0.0) for k in range(n_kv)], axis=0
            )
            high = spread.astype(jnp.bfloat16)
            low = (spread - high.astype(jnp.float32)).astype(jnp.bfloat16)
            fresh_spread = jnp.where(own_kv, fresh_weight, 0.0)
            fresh_high = fresh_spread.astype(jnp.bfloat16)
            fresh_low = (fresh_spread - fresh_high.astype(jnp.float32)).astype(jnp.bfloat16)
            fresh_value = jnp.concatenate(
                [new_ref[r : r + 1, 1, HD * k : HD * (k + 1)] for k in range(n_kv)], axis=0
            )
            both = ((0,), (0,))
            summed = contract(high, values, both) + contract(low, values, both)
            summed = summed + (
                contract(fresh_high, fresh_value, both) + contract(fresh_low, fresh_value, both)
            )
            out_ref[r, 0:n_heads, :] = summed.astype(jnp.bfloat16)
            parts = split3(peak) + split3(total)
            pad = jnp.zeros((STAT_ROWS - len(parts), n_heads), jnp.float32)
            stats = jnp.concatenate([part.astype(jnp.float32) for part in parts] + [pad], axis=0)
            out_ref[r, n_heads : n_heads + STAT_ROWS, :] = stats.astype(jnp.bfloat16)
        for copy in fetch_wo:
            copy.wait()

    in_vmem, in_hbm = pl.BlockSpec(memory_space=VMEM), pl.BlockSpec(memory_space=HBM)
    return pl.pallas_call(
        body,
        out_shape=(
            jax.ShapeDtypeStruct((n_rows, n_heads + STAT_ROWS, HD), jnp.bfloat16),
            pltpu.VMEM((n_early, wo.shape[0], piece), wo.dtype),
        ),
        in_specs=[pl.BlockSpec(memory_space=SMEM)]
        + [in_vmem] * 3 + [in_hbm] * 2 + [in_vmem] * 2 + [in_hbm],
        out_specs=(in_vmem, in_vmem),
        scratch_shapes=[
            pltpu.VMEM((n_rows * n_heads, HD), jnp.float32),
            pltpu.VMEM((n_rows * n_kv, HD), jnp.float32),
            pltpu.VMEM(new_kv.shape, new_kv.dtype),
            pltpu.VMEM(kv_codes.shape, kv_codes.dtype),
            pltpu.SemaphoreType.DMA,
            pltpu.SemaphoreType.DMA((n_rows,)),
            pltpu.SemaphoreType.DMA((n_early,)),
        ],
        compiler_params=pltpu.CompilerParams(vmem_limit_bytes=12 * MIB),
        name="attend",
    )(scalars, gathered, cosine, sine, new_kv, kv_codes, key_scales, value_scales, wo)


def settle(main, stats, n_heads, stat_row, n_target, copies):
    n_src = main.shape[0]
    depth = main.shape[2]
    heads_root = n_heads ** (-0.5)
    heads_out = n_heads // n_target
    n_out = n_target * len(copies(0))

    def body(main_ref, stat_ref, out_ref):
        peaks, totals = [], []
        for b in range(n_src):
            part = stat_ref[b, stat_row : stat_row + STAT_ROWS, :].astype(jnp.float32)
            peaks.append(part[0:1] + part[1:2] + part[2:3])
            totals.append(part[3:4] + part[4:5] + part[5:6])
        peak = functools.reduce(jnp.maximum, peaks)
        scales = [jnp.exp(p - peak) for p in peaks]
        total = functools.reduce(jnp.add, [s * t for s, t in zip(scales, totals)])
        common = lax.broadcasted_iota(jnp.int32, (n_heads, n_heads), 0) & lax.broadcasted_iota(
            jnp.int32, (n_heads, n_heads), 1
        )
        bits = (n_heads - 1).bit_length()
        parity = common
        for bit in range(1, bits):
            parity = parity ^ (common >> bit)
        sign = jnp.where((parity & 1) == 0, heads_root, -heads_root)
        acc = jnp.zeros((n_heads, depth), jnp.float32)
        for b in range(n_src):
            mixed = sign * (scales[b] / total)
            high = mixed.astype(jnp.bfloat16)
            low = (mixed - high.astype(jnp.float32)).astype(jnp.bfloat16)
            value = main_ref[b, 0:n_heads, :]
            acc = acc + jnp.dot(high, value, preferred_element_type=jnp.float32)
            acc = acc + jnp.dot(low, value, preferred_element_type=jnp.float32)
        rotated = acc.astype(jnp.bfloat16)
        for h in range(n_target):
            for spot in copies(h):
                out_ref[spot] = rotated[h * heads_out : (h + 1) * heads_out]

    return pl.pallas_call(
        body,
        out_shape=jax.ShapeDtypeStruct((n_out, heads_out, depth), jnp.bfloat16),
        in_specs=[pl.BlockSpec(memory_space=VMEM)] * 2,
        out_specs=pl.BlockSpec(memory_space=VMEM),
        compiler_params=pltpu.CompilerParams(vmem_limit_bytes=16 * MIB),
        name="settle",
    )(main, stats)


def project(own_share, rows, early, wo, n_block, tiles, spot):
    n_all, heads_here, _ = rows.shape
    n_early, depth, piece = early.shape
    n_late = n_block - n_early
    n_rows = n_all // len(tiles)

    def body(own_ref, x_ref, early_ref, wo_ref, out_ref, late, wide, packed, sem):
        fetch = weight_fetch(wo_ref, late, sem, own_ref[0], n_block, piece)
        fetch_wo = [fetch(n_early + b, b) for b in range(n_late)]
        for copy in fetch_wo:
            copy.start()
        wide[...] = x_ref[...].astype(jnp.float32).reshape(n_all * heads_here, HD)
        for j in range(heads_here):
            pieces = [
                wide[pl.ds(first * heads_here + j, n_rows, stride=heads_here * step), :]
                for first, step in tiles
            ]
            packed[:, HD * j : HD * (j + 1)] = jnp.concatenate(pieces, axis=0).astype(jnp.bfloat16)
        x = packed[...]
        for b in range(n_block):
            if b < n_early:
                block = early_ref[b]
            else:
                fetch_wo[b - n_early].wait()
                block = late[b - n_early]
            share = jnp.dot(x, block, preferred_element_type=jnp.float32)
            for s in range(len(tiles)):
                out_ref[spot(b, s)] = share[s * n_rows : (s + 1) * n_rows].astype(jnp.bfloat16)

    in_vmem = pl.BlockSpec(memory_space=VMEM)
    return pl.pallas_call(
        body,
        out_shape=jax.ShapeDtypeStruct((n_block * len(tiles), n_rows, piece), jnp.bfloat16),
        in_specs=[
            pl.BlockSpec(memory_space=SMEM), in_vmem, in_vmem, pl.BlockSpec(memory_space=HBM)
        ],
        out_specs=in_vmem,
        scratch_shapes=[
            pltpu.VMEM((n_late, depth, piece), wo.dtype),
            pltpu.VMEM((n_all * heads_here, HD), jnp.float32),
            pltpu.VMEM((n_all, heads_here * HD), jnp.bfloat16),
            pltpu.SemaphoreType.DMA((n_late,)),
        ],
        compiler_params=pltpu.CompilerParams(vmem_limit_bytes=24 * MIB),
        name="project",
    )(own_share, rows, early, wo)


def finish(shares, scales, residual, n_head, n_share, spot):
    piece = shares.shape[2]

    def body(share_ref, scale_ref, res_ref, out_ref):
        for s in range(n_share):
            total = share_ref[spot(0, s)].astype(jnp.float32)
            for h in range(1, n_head):
                total = total + share_ref[spot(h, s)].astype(jnp.float32)
            cols = slice(s * piece, (s + 1) * piece)
            out_ref[:, cols] = (
                res_ref[:, cols].astype(jnp.float32) + total * scale_ref[:, cols]
            ).astype(jnp.bfloat16)

    return pl.pallas_call(
        body,
        out_shape=jax.ShapeDtypeStruct(residual.shape, jnp.bfloat16),
        in_specs=[pl.BlockSpec(memory_space=VMEM)] * 3,
        out_specs=pl.BlockSpec(memory_space=VMEM),
        compiler_params=pltpu.CompilerParams(vmem_limit_bytes=16 * MIB),
        name="finish",
    )(shares, scales, residual)


def exchange(block, axes):
    return lax.all_to_all(block, axes, split_axis=0, concat_axis=0, tiled=True)


def on_device(
    queries, new_kv, positions, lengths, kv_codes, kv_scales, wo_codes, wo_scales, residual
):
    n_head = lax.axis_size("head")
    n_dp = lax.axis_size("dp")
    my_head = lax.axis_index("head")
    n_rows, width = queries.shape
    heads_here = width // HD
    n_heads = heads_here * n_head
    n_kv = new_kv.shape[2] // HD
    block_len = kv_codes.shape[2]
    own_cols = wo_codes.shape[1] // n_head
    n_group = lax.axis_size("group")
    if own_cols % (n_group * n_dp * 128):
        n_group = 1
    n_share = n_group * n_dp
    piece = own_cols // n_share
    my_share = lax.axis_index("dp")
    axes = ("head", "dp")
    if n_group > 1:
        my_share = my_share + n_dp * lax.axis_index("group")
        axes = ("group", "head", "dp")

    def spot(head, share):
        return (share // n_dp * n_head + head) * n_dp + share % n_dp

    gathered = exchange(jnp.broadcast_to(queries, (n_head, n_rows, width)), "head")
    cosine, sine = rotary_tables(positions)
    spread = jnp.repeat(jnp.swapaxes(kv_scales, 2, 3), n_heads // n_kv, axis=3)
    own_share = my_share.reshape(1).astype(jnp.int32)
    first_slot = (my_head * block_len).reshape(1).astype(jnp.int32)
    scalars, own_share, gathered, cosine, sine, spread = lax.optimization_barrier(
        (jnp.concatenate([lengths, first_slot, own_share]), own_share, gathered, cosine, sine, spread)
    )
    partial, early = attend(
        scalars, gathered, cosine, sine, new_kv, kv_codes, spread[:, 0], spread[:, 1], wo_codes,
        n_head // 2, piece,
    )

    cuts = max(1, n_head // n_rows)
    depth = HD // cuts
    if cuts == 1:
        main = exchange(partial, "head")
        stats, stat_row = main, n_heads
    else:
        values = partial[:, :n_heads].reshape(n_rows, n_heads, cuts, depth).swapaxes(1, 2)
        stats = partial[:, n_heads:].reshape(n_rows, 1, STAT_ROWS * cuts, depth)
        stats = jnp.broadcast_to(stats, (n_rows, cuts) + stats.shape[2:])
        message = jnp.concatenate([values, stats], axis=2)
        received = exchange(message.reshape((n_head,) + message.shape[2:]), "head")
        main, stat_row = received[:, :n_heads], 0
        stats = received[:, n_heads:].reshape(n_head, STAT_ROWS, HD)
    copies = settle(
        main, stats, n_heads, stat_row, n_head, lambda h: [spot(h, s) for s in range(n_share)]
    )
    rows = exchange(copies, axes)
    if cuts > 1:
        rows = rows.reshape(n_group, n_rows, cuts, n_dp, heads_here, depth)
        rows = rows.transpose(0, 1, 3, 4, 2, 5).reshape(n_rows * n_share, heads_here, HD)
    tiles = [(s // n_dp * n_rows * n_dp + s % n_dp, n_dp) for s in range(n_share)]
    shares = exchange(project(own_share, rows, early, wo_codes, n_head, tiles, spot), axes)
    return finish(shares, wo_scales.reshape(1, own_cols), residual, n_head, n_share, spot)


def solution(mesh):
    placed = (
        P(("group", "dp"), "head"),
        P(("group", "dp"), None, None),
        P(("group", "dp")),
        P(("group", "dp")),
        P(("group", "dp"), None, "head", None),
        P(("group", "dp"), None, None, "head"),
        P("head", None),
        P("head"),
        P(("group", "dp"), "head"),
    )
    return jax.shard_map(
        on_device, mesh=mesh, in_specs=placed, out_specs=P(("group", "dp"), "head"), check_vma=False
    )
```

```python
import functools
import jax
import jax.numpy as jnp
from jax import lax
from jax.experimental import pallas as pl
from jax.experimental.pallas import tpu as pltpu
from jax.sharding import PartitionSpec as P

HD = 128
ROPE_BASE = 500000.0
NEG_FILL = -1e30
STAT_ROWS = 8
MIB = 1 << 20
VMEM = pltpu.MemorySpace.VMEM
SMEM = pltpu.MemorySpace.SMEM
HBM = pltpu.MemorySpace.HBM


def split3(value):
    high = value.astype(jnp.bfloat16)
    rest = value - high.astype(jnp.float32)
    middle = rest.astype(jnp.bfloat16)
    low = (rest - middle.astype(jnp.float32)).astype(jnp.bfloat16)
    return high, middle, low


def contract(left, right, dims):
    return lax.dot_general(left, right, (dims, ((), ())), preferred_element_type=jnp.float32)


def in_place(array):
    return pltpu.with_memory_space_constraint(array, HBM)


def rotary_tables(positions):
    half_dim = HD // 2
    inverse_rate = ROPE_BASE ** (-(jnp.arange(half_dim, dtype=jnp.float32) * (2.0 / HD)))
    angles = positions.astype(jnp.float32)[:, None] * inverse_rate
    cosine = jnp.cos(angles)
    sine = jnp.sin(angles)
    return jnp.concatenate([cosine, cosine], -1), jnp.concatenate([-sine, sine], -1)


def stage(arrays):
    def body(*refs):
        count = len(arrays)
        copies = [
            pltpu.make_async_copy(refs[n], refs[count + n], refs[-1].at[n]) for n in range(count)
        ]
        for copy in copies:
            copy.start()
        for copy in copies:
            copy.wait()

    in_hbm, in_vmem = pl.BlockSpec(memory_space=HBM), pl.BlockSpec(memory_space=VMEM)
    return pl.pallas_call(
        body,
        out_shape=tuple(pltpu.VMEM(a.shape, a.dtype) for a in arrays),
        in_specs=[in_hbm] * len(arrays),
        out_specs=(in_vmem,) * len(arrays),
        scratch_shapes=[pltpu.SemaphoreType.DMA((len(arrays),))],
        compiler_params=pltpu.CompilerParams(vmem_limit_bytes=MIB // 4),
        name="stage",
    )(*[in_place(a) for a in arrays])


def attend(
    scalars, gathered, cosine, sine, new_kv, kv_codes, key_scales, value_scales
):
    n_src, n_rows, width = gathered.shape
    heads_here = width // HD
    n_heads = n_src * heads_here
    block_len = kv_codes.shape[2]
    n_kv = kv_codes.shape[3] // HD
    group = n_heads // n_kv
    score_scale = HD ** (-0.5)

    def body(s_ref, q_ref, cos_ref, sin_ref, new_ref, kv_ref, ks_ref, vs_ref, out_ref, qs, ks):
        cos, sin = cos_ref[...], sin_ref[...]

        def rotate(tile):
            return tile * cos + pltpu.roll(tile, HD // 2, 1) * sin

        for src in range(n_src):
            block = q_ref[src].astype(jnp.float32)
            for j in range(heads_here):
                head = src * heads_here + j
                qs[n_rows * head : n_rows * (head + 1), :] = rotate(block[:, HD * j : HD * (j + 1)])
        fresh = new_ref[:, 0, :].astype(jnp.float32)
        for k in range(n_kv):
            ks[n_rows * k : n_rows * (k + 1), :] = rotate(fresh[:, HD * k : HD * (k + 1)])

        first_slot = s_ref[n_rows]
        is_first = first_slot == 0
        lane_group = lax.broadcasted_iota(jnp.int32, (1, n_heads), 1) // group
        slot = first_slot + lax.broadcasted_iota(jnp.int32, (block_len, n_heads), 0)
        own_kv = lax.broadcasted_iota(jnp.int32, (n_kv, n_heads), 0) == lane_group
        for r in range(n_rows):
            query = qs[pl.ds(r, n_heads, stride=n_rows), :].astype(jnp.bfloat16)
            keys = jnp.concatenate(
                [kv_ref[r, 0, :, HD * k : HD * (k + 1)] for k in range(n_kv)], axis=0
            )
            values = jnp.concatenate(
                [kv_ref[r, 1, :, HD * k : HD * (k + 1)] for k in range(n_kv)], axis=0
            )
            raw = contract(keys, query, ((1,), (1,)))
            raw_own = jnp.zeros((block_len, n_heads), jnp.float32)
            for k in range(n_kv):
                raw_own = jnp.where(lane_group == k, raw[block_len * k : block_len * (k + 1)], raw_own)
            is_valid = slot < s_ref[r]
            scores = jnp.where(is_valid, raw_own * ks_ref[r] * score_scale, NEG_FILL)
            fresh_key = ks[pl.ds(r, n_kv, stride=n_rows), :].astype(jnp.bfloat16)
            fresh_raw = contract(fresh_key, query, ((1,), (1,)))
            fresh_score = jnp.sum(jnp.where(own_kv, fresh_raw, 0.0), axis=0, keepdims=True) * score_scale
            fresh_score = jnp.where(is_first, fresh_score, NEG_FILL)
            peak = jnp.maximum(jnp.max(scores, axis=0, keepdims=True), fresh_score)
            weights = jnp.where(is_valid, jnp.exp(scores - peak), 0.0)
            fresh_weight = jnp.where(is_first, jnp.exp(fresh_score - peak), 0.0)
            total = jnp.sum(weights, axis=0, keepdims=True) + fresh_weight
            scaled = weights * vs_ref[r]
            spread = jnp.concatenate(
                [jnp.where(lane_group == k, scaled, 0.0) for k in range(n_kv)], axis=0
            )
            high = spread.astype(jnp.bfloat16)
            low = (spread - high.astype(jnp.float32)).astype(jnp.bfloat16)
            fresh_spread = jnp.where(own_kv, fresh_weight, 0.0)
            fresh_high = fresh_spread.astype(jnp.bfloat16)
            fresh_low = (fresh_spread - fresh_high.astype(jnp.float32)).astype(jnp.bfloat16)
            fresh_value = jnp.concatenate(
                [new_ref[r : r + 1, 1, HD * k : HD * (k + 1)] for k in range(n_kv)], axis=0
            )
            both = ((0,), (0,))
            summed = contract(high, values, both) + contract(low, values, both)
            summed = summed + (
                contract(fresh_high, fresh_value, both) + contract(fresh_low, fresh_value, both)
            )
            out_ref[r, 0:n_heads, :] = summed.astype(jnp.bfloat16)
            parts = split3(peak) + split3(total)
            pad = jnp.zeros((STAT_ROWS - len(parts), n_heads), jnp.float32)
            stats = jnp.concatenate([part.astype(jnp.float32) for part in parts] + [pad], axis=0)
            out_ref[r, n_heads : n_heads + STAT_ROWS, :] = stats.astype(jnp.bfloat16)

    in_vmem = pl.BlockSpec(memory_space=VMEM)
    return pl.pallas_call(
        body,
        out_shape=jax.ShapeDtypeStruct((n_rows, n_heads + STAT_ROWS, HD), jnp.bfloat16),
        in_specs=[pl.BlockSpec(memory_space=SMEM)] + [in_vmem] * 7,
        out_specs=in_vmem,
        scratch_shapes=[
            pltpu.VMEM((n_rows * n_heads, HD), jnp.float32),
            pltpu.VMEM((n_rows * n_kv, HD), jnp.float32),
        ],
        compiler_params=pltpu.CompilerParams(vmem_limit_bytes=6 * MIB),
        name="attend",
    )(scalars, gathered, cosine, sine, new_kv, kv_codes, key_scales, value_scales)


def settle(main, stats, n_heads, stat_row, n_target, copies):
    n_src = main.shape[0]
    depth = main.shape[2]
    heads_root = n_heads ** (-0.5)
    heads_out = n_heads // n_target
    n_out = n_target * len(copies(0))

    def body(main_ref, stat_ref, out_ref):
        peaks, totals = [], []
        for b in range(n_src):
            part = stat_ref[b, stat_row : stat_row + STAT_ROWS, :].astype(jnp.float32)
            peaks.append(part[0:1] + part[1:2] + part[2:3])
            totals.append(part[3:4] + part[4:5] + part[5:6])
        peak = functools.reduce(jnp.maximum, peaks)
        scales = [jnp.exp(p - peak) for p in peaks]
        total = functools.reduce(jnp.add, [s * t for s, t in zip(scales, totals)])
        common = lax.broadcasted_iota(jnp.int32, (n_heads, n_heads), 0) & lax.broadcasted_iota(
            jnp.int32, (n_heads, n_heads), 1
        )
        bits = (n_heads - 1).bit_length()
        parity = common
        for bit in range(1, bits):
            parity = parity ^ (common >> bit)
        sign = jnp.where((parity & 1) == 0, heads_root, -heads_root)
        acc = jnp.zeros((n_heads, depth), jnp.float32)
        for b in range(n_src):
            mixed = sign * (scales[b] / total)
            high = mixed.astype(jnp.bfloat16)
            low = (mixed - high.astype(jnp.float32)).astype(jnp.bfloat16)
            value = main_ref[b, 0:n_heads, :]
            acc = acc + jnp.dot(high, value, preferred_element_type=jnp.float32)
            acc = acc + jnp.dot(low, value, preferred_element_type=jnp.float32)
        rotated = acc.astype(jnp.bfloat16)
        for h in range(n_target):
            for spot in copies(h):
                out_ref[spot] = rotated[h * heads_out : (h + 1) * heads_out]

    return pl.pallas_call(
        body,
        out_shape=jax.ShapeDtypeStruct((n_out, heads_out, depth), jnp.bfloat16),
        in_specs=[pl.BlockSpec(memory_space=VMEM)] * 2,
        out_specs=pl.BlockSpec(memory_space=VMEM),
        compiler_params=pltpu.CompilerParams(vmem_limit_bytes=16 * MIB),
        name="settle",
    )(main, stats)


def project(own_share, rows, wo, n_block, tiles, spot):
    n_all, heads_here, _ = rows.shape
    depth = wo.shape[0]
    block_cols = wo.shape[1] // n_block
    piece = block_cols // len(tiles)
    n_rows = n_all // len(tiles)

    def body(own_ref, x_ref, wo_ref, out_ref, weights, wide, packed, sem):
        def fetch(b):
            cols = pl.ds(pl.multiple_of(b * block_cols + own_ref[0] * piece, 128), piece)
            return pltpu.make_async_copy(wo_ref.at[:, cols], weights.at[b], sem.at[b])

        for b in range(n_block):
            fetch(b).start()
        wide[...] = x_ref[...].astype(jnp.float32).reshape(n_all * heads_here, HD)
        for j in range(heads_here):
            pieces = [
                wide[pl.ds(first * heads_here + j, n_rows, stride=heads_here * step), :]
                for first, step in tiles
            ]
            packed[:, HD * j : HD * (j + 1)] = jnp.concatenate(pieces, axis=0).astype(jnp.bfloat16)
        x = packed[...]
        for b in range(n_block):
            fetch(b).wait()
            share = jnp.dot(x, weights[b], preferred_element_type=jnp.float32)
            for s in range(len(tiles)):
                out_ref[spot(b, s)] = share[s * n_rows : (s + 1) * n_rows].astype(jnp.bfloat16)

    in_vmem = pl.BlockSpec(memory_space=VMEM)
    return pl.pallas_call(
        body,
        out_shape=jax.ShapeDtypeStruct((n_block * len(tiles), n_rows, piece), jnp.bfloat16),
        in_specs=[pl.BlockSpec(memory_space=SMEM), in_vmem, pl.BlockSpec(memory_space=HBM)],
        out_specs=in_vmem,
        scratch_shapes=[
            pltpu.VMEM((n_block, depth, piece), wo.dtype),
            pltpu.VMEM((n_all * heads_here, HD), jnp.float32),
            pltpu.VMEM((n_all, heads_here * HD), jnp.bfloat16),
            pltpu.SemaphoreType.DMA((n_block,)),
        ],
        compiler_params=pltpu.CompilerParams(vmem_limit_bytes=24 * MIB),
        name="project",
    )(own_share, rows, in_place(wo))


def finish(shares, scales, residual, n_head, n_share, spot):
    piece = shares.shape[2]

    def body(share_ref, scale_ref, res_ref, out_ref):
        for s in range(n_share):
            total = share_ref[spot(0, s)].astype(jnp.float32)
            for h in range(1, n_head):
                total = total + share_ref[spot(h, s)].astype(jnp.float32)
            cols = slice(s * piece, (s + 1) * piece)
            out_ref[:, cols] = (
                res_ref[:, cols].astype(jnp.float32) + total * scale_ref[:, cols]
            ).astype(jnp.bfloat16)

    return pl.pallas_call(
        body,
        out_shape=jax.ShapeDtypeStruct(residual.shape, jnp.bfloat16),
        in_specs=[pl.BlockSpec(memory_space=VMEM)] * 3,
        out_specs=pl.BlockSpec(memory_space=VMEM),
        compiler_params=pltpu.CompilerParams(vmem_limit_bytes=16 * MIB),
        name="finish",
    )(shares, scales, residual)


def exchange(block, axes):
    return lax.all_to_all(block, axes, split_axis=0, concat_axis=0, tiled=True)


def on_device(
    queries, new_kv, positions, lengths, kv_codes, kv_scales, wo_codes, wo_scales, residual
):
    n_head = lax.axis_size("head")
    n_dp = lax.axis_size("dp")
    my_head = lax.axis_index("head")
    n_rows, width = queries.shape
    heads_here = width // HD
    n_heads = heads_here * n_head
    n_kv = new_kv.shape[2] // HD
    block_len = kv_codes.shape[2]
    own_cols = wo_codes.shape[1] // n_head
    n_group = lax.axis_size("group")
    if own_cols % (n_group * n_dp * 128):
        n_group = 1
    n_share = n_group * n_dp
    piece = own_cols // n_share
    my_share = lax.axis_index("dp")
    axes = ("head", "dp")
    if n_group > 1:
        my_share = my_share + n_dp * lax.axis_index("group")
        axes = ("group", "head", "dp")

    def spot(head, share):
        return (share // n_dp * n_head + head) * n_dp + share % n_dp

    gathered = exchange(jnp.broadcast_to(queries, (n_head, n_rows, width)), "head")
    cosine, sine = rotary_tables(positions)
    spread = jnp.repeat(jnp.swapaxes(kv_scales, 2, 3), n_heads // n_kv, axis=3)
    own_share = my_share.reshape(1).astype(jnp.int32)
    first_slot = (my_head * block_len).reshape(1).astype(jnp.int32)
    scalars = jnp.concatenate([lengths, first_slot])
    new_staged, kv_staged = stage((new_kv, kv_codes))
    partial = attend(
        scalars, gathered, cosine, sine, new_staged, kv_staged, spread[:, 0], spread[:, 1]
    )
    own_share, partial = lax.optimization_barrier((own_share, partial))

    cuts = max(1, n_head // n_rows)
    depth = HD // cuts
    if cuts == 1:
        main = exchange(partial, "head")
        stats, stat_row = main, n_heads
    else:
        values = partial[:, :n_heads].reshape(n_rows, n_heads, cuts, depth).swapaxes(1, 2)
        stats = partial[:, n_heads:].reshape(n_rows, 1, STAT_ROWS * cuts, depth)
        stats = jnp.broadcast_to(stats, (n_rows, cuts) + stats.shape[2:])
        message = jnp.concatenate([values, stats], axis=2)
        received = exchange(message.reshape((n_head,) + message.shape[2:]), "head")
        main, stat_row = received[:, :n_heads], 0
        stats = received[:, n_heads:].reshape(n_head, STAT_ROWS, HD)
    copies = settle(
        main, stats, n_heads, stat_row, n_head, lambda h: [spot(h, s) for s in range(n_share)]
    )
    rows = exchange(copies, axes)
    if cuts > 1:
        rows = rows.reshape(n_group, n_rows, cuts, n_dp, heads_here, depth)
        rows = rows.transpose(0, 1, 3, 4, 2, 5).reshape(n_rows * n_share, heads_here, HD)
    tiles = [(s // n_dp * n_rows * n_dp + s % n_dp, n_dp) for s in range(n_share)]
    shares = exchange(project(own_share, rows, wo_codes, n_head, tiles, spot), axes)
    return finish(shares, wo_scales.reshape(1, own_cols), residual, n_head, n_share, spot)


def solution(mesh):
    placed = (
        P(("group", "dp"), "head"),
        P(("group", "dp"), None, None),
        P(("group", "dp")),
        P(("group", "dp")),
        P(("group", "dp"), None, "head", None),
        P(("group", "dp"), None, None, "head"),
        P("head", None),
        P("head"),
        P(("group", "dp"), "head"),
    )
    return jax.shard_map(
        on_device, mesh=mesh, in_specs=placed, out_specs=P(("group", "dp"), "head"), check_vma=False
    )
```

```python
import functools
import jax
import jax.numpy as jnp
from jax import lax
from jax.experimental import pallas as pl
from jax.experimental.pallas import tpu as pltpu
from jax.sharding import PartitionSpec as P

HD = 128
ROPE_BASE = 500000.0
NEG_FILL = -1e30
STAT_ROWS = 8
ROW_UNROLL = 4
EARLY_EIGHTHS = 3
MIB = 1 << 20
VMEM = pltpu.MemorySpace.VMEM
SMEM = pltpu.MemorySpace.SMEM
HBM = pltpu.MemorySpace.HBM


def split3(value):
    high = value.astype(jnp.bfloat16)
    rest = value - high.astype(jnp.float32)
    middle = rest.astype(jnp.bfloat16)
    low = (rest - middle.astype(jnp.float32)).astype(jnp.bfloat16)
    return high, middle, low


def contract(left, right, dims):
    return lax.dot_general(left, right, (dims, ((), ())), preferred_element_type=jnp.float32)


def in_place(array):
    return pltpu.with_memory_space_constraint(array, HBM)


def rotary_tables(positions):
    half_dim = HD // 2
    inverse_rate = ROPE_BASE ** (-(jnp.arange(half_dim, dtype=jnp.float32) * (2.0 / HD)))
    angles = positions.astype(jnp.float32)[:, None] * inverse_rate
    cosine = jnp.cos(angles)
    sine = jnp.sin(angles)
    return jnp.concatenate([cosine, cosine], -1), jnp.concatenate([-sine, sine], -1)


def stage(arrays):
    def body(*refs):
        count = len(arrays)
        copies = [
            pltpu.make_async_copy(refs[n], refs[count + n], refs[-1].at[n]) for n in range(count)
        ]
        for copy in copies:
            copy.start()
        for copy in copies:
            copy.wait()

    in_hbm, in_vmem = pl.BlockSpec(memory_space=HBM), pl.BlockSpec(memory_space=VMEM)
    return pl.pallas_call(
        body,
        out_shape=tuple(pltpu.VMEM(a.shape, a.dtype) for a in arrays),
        in_specs=[in_hbm] * len(arrays),
        out_specs=(in_vmem,) * len(arrays),
        scratch_shapes=[pltpu.SemaphoreType.DMA((len(arrays),))],
        compiler_params=pltpu.CompilerParams(vmem_limit_bytes=MIB // 4),
        name="stage",
    )(*[in_place(a) for a in arrays])


def weight_fetch(wo_ref, out_ref, sem, share, n_block, piece):
    def fetch(block, slot):
        start = block * (wo_ref.shape[1] // n_block) + share * piece
        cols = pl.ds(pl.multiple_of(start, 128), piece)
        return pltpu.make_async_copy(wo_ref.at[:, cols], out_ref.at[slot], sem.at[slot])

    return fetch


def attend(
    scalars, gathered, cosine, sine, new_kv, kv_codes, key_scales, value_scales, wo, n_early, piece
):
    n_src, n_rows, width = gathered.shape
    heads_here = width // HD
    n_heads = n_src * heads_here
    block_len = kv_codes.shape[2]
    n_kv = kv_codes.shape[3] // HD
    group = n_heads // n_kv
    score_scale = HD ** (-0.5)

    def body(
        s_ref, q_ref, cos_ref, sin_ref, new_ref, kv_ref, ks_ref, vs_ref, wo_ref, out_ref, early_ref,
        qs, ks, wo_sem,
    ):
        fetch = weight_fetch(wo_ref, early_ref, wo_sem, s_ref[n_rows + 1], n_src, piece)
        fetch_wo = [fetch(b, b) for b in range(n_early)]
        for copy in fetch_wo:
            copy.start()
        cos, sin = cos_ref[...], sin_ref[...]

        def rotate(tile):
            return tile * cos + pltpu.roll(tile, HD // 2, 1) * sin

        for src in range(n_src):
            block = q_ref[src].astype(jnp.float32)
            for j in range(heads_here):
                head = src * heads_here + j
                qs[n_rows * head : n_rows * (head + 1), :] = rotate(block[:, HD * j : HD * (j + 1)])
        fresh = new_ref[:, 0, :].astype(jnp.float32)
        for k in range(n_kv):
            ks[n_rows * k : n_rows * (k + 1), :] = rotate(fresh[:, HD * k : HD * (k + 1)])

        first_slot = s_ref[n_rows]
        is_first = first_slot == 0
        lane_group = lax.broadcasted_iota(jnp.int32, (1, n_heads), 1) // group
        slot = first_slot + lax.broadcasted_iota(jnp.int32, (block_len, n_heads), 0)
        own_kv = lax.broadcasted_iota(jnp.int32, (n_kv, n_heads), 0) == lane_group
        def one_row(r):
            query = qs[pl.ds(r, n_heads, stride=n_rows), :].astype(jnp.bfloat16)
            keys = jnp.concatenate(
                [kv_ref[r, 0, :, HD * k : HD * (k + 1)] for k in range(n_kv)], axis=0
            )
            values = jnp.concatenate(
                [kv_ref[r, 1, :, HD * k : HD * (k + 1)] for k in range(n_kv)], axis=0
            )
            raw = contract(keys, query, ((1,), (1,)))
            raw_own = jnp.zeros((block_len, n_heads), jnp.float32)
            for k in range(n_kv):
                raw_own = jnp.where(lane_group == k, raw[block_len * k : block_len * (k + 1)], raw_own)
            is_valid = slot < s_ref[r]
            scores = jnp.where(is_valid, raw_own * ks_ref[r] * score_scale, NEG_FILL)
            fresh_key = ks[pl.ds(r, n_kv, stride=n_rows), :].astype(jnp.bfloat16)
            fresh_raw = contract(fresh_key, query, ((1,), (1,)))
            fresh_score = jnp.sum(jnp.where(own_kv, fresh_raw, 0.0), axis=0, keepdims=True) * score_scale
            fresh_score = jnp.where(is_first, fresh_score, NEG_FILL)
            peak = jnp.maximum(jnp.max(scores, axis=0, keepdims=True), fresh_score)
            weights = jnp.where(is_valid, jnp.exp(scores - peak), 0.0)
            fresh_weight = jnp.where(is_first, jnp.exp(fresh_score - peak), 0.0)
            total = jnp.sum(weights, axis=0, keepdims=True) + fresh_weight
            scaled = weights * vs_ref[r]
            spread = jnp.concatenate(
                [jnp.where(lane_group == k, scaled, 0.0) for k in range(n_kv)], axis=0
            )
            high = spread.astype(jnp.bfloat16)
            low = (spread - high.astype(jnp.float32)).astype(jnp.bfloat16)
            fresh_spread = jnp.where(own_kv, fresh_weight, 0.0)
            fresh_high = fresh_spread.astype(jnp.bfloat16)
            fresh_low = (fresh_spread - fresh_high.astype(jnp.float32)).astype(jnp.bfloat16)
            fresh_value = jnp.concatenate(
                [new_ref[pl.ds(r, 1), 1, HD * k : HD * (k + 1)] for k in range(n_kv)], axis=0
            )
            both = ((0,), (0,))
            summed = contract(high, values, both) + contract(low, values, both)
            summed = summed + (
                contract(fresh_high, fresh_value, both) + contract(fresh_low, fresh_value, both)
            )
            out_ref[r, 0:n_heads, :] = summed.astype(jnp.bfloat16)
            parts = split3(peak) + split3(total)
            pad = jnp.zeros((STAT_ROWS - len(parts), n_heads), jnp.float32)
            stats = jnp.concatenate([part.astype(jnp.float32) for part in parts] + [pad], axis=0)
            out_ref[r, n_heads : n_heads + STAT_ROWS, :] = stats.astype(jnp.bfloat16)

        def some_rows(step, carry):
            for u in range(ROW_UNROLL):
                one_row(step * ROW_UNROLL + u)
            return carry

        lax.fori_loop(0, n_rows // ROW_UNROLL, some_rows, 0)
        for copy in fetch_wo:
            copy.wait()

    in_vmem = pl.BlockSpec(memory_space=VMEM)
    return pl.pallas_call(
        body,
        out_shape=(
            jax.ShapeDtypeStruct((n_rows, n_heads + STAT_ROWS, HD), jnp.bfloat16),
            pltpu.VMEM((n_early, wo.shape[0], piece), wo.dtype),
        ),
        in_specs=[pl.BlockSpec(memory_space=SMEM)]
        + [in_vmem] * 7 + [pl.BlockSpec(memory_space=HBM)],
        out_specs=(in_vmem, in_vmem),
        scratch_shapes=[
            pltpu.VMEM((n_rows * n_heads, HD), jnp.float32),
            pltpu.VMEM((n_rows * n_kv, HD), jnp.float32),
            pltpu.SemaphoreType.DMA((n_early,)),
        ],
        compiler_params=pltpu.CompilerParams(vmem_limit_bytes=6 * MIB),
        name="attend",
    )(
        scalars, gathered, cosine, sine, new_kv, kv_codes, key_scales, value_scales, in_place(wo)
    )


def settle(main, stats, n_heads, stat_row, n_target, copies):
    n_src = main.shape[0]
    depth = main.shape[2]
    heads_root = n_heads ** (-0.5)
    heads_out = n_heads // n_target
    n_out = n_target * len(copies(0))

    def body(main_ref, stat_ref, out_ref):
        peaks, totals = [], []
        for b in range(n_src):
            part = stat_ref[b, stat_row : stat_row + STAT_ROWS, :].astype(jnp.float32)
            peaks.append(part[0:1] + part[1:2] + part[2:3])
            totals.append(part[3:4] + part[4:5] + part[5:6])
        peak = functools.reduce(jnp.maximum, peaks)
        scales = [jnp.exp(p - peak) for p in peaks]
        total = functools.reduce(jnp.add, [s * t for s, t in zip(scales, totals)])
        common = lax.broadcasted_iota(jnp.int32, (n_heads, n_heads), 0) & lax.broadcasted_iota(
            jnp.int32, (n_heads, n_heads), 1
        )
        bits = (n_heads - 1).bit_length()
        parity = common
        for bit in range(1, bits):
            parity = parity ^ (common >> bit)
        sign = jnp.where((parity & 1) == 0, heads_root, -heads_root)
        acc = jnp.zeros((n_heads, depth), jnp.float32)
        for b in range(n_src):
            mixed = sign * (scales[b] / total)
            high = mixed.astype(jnp.bfloat16)
            low = (mixed - high.astype(jnp.float32)).astype(jnp.bfloat16)
            value = main_ref[b, 0:n_heads, :]
            acc = acc + jnp.dot(high, value, preferred_element_type=jnp.float32)
            acc = acc + jnp.dot(low, value, preferred_element_type=jnp.float32)
        rotated = acc.astype(jnp.bfloat16)
        for h in range(n_target):
            for spot in copies(h):
                out_ref[spot] = rotated[h * heads_out : (h + 1) * heads_out]

    return pl.pallas_call(
        body,
        out_shape=jax.ShapeDtypeStruct((n_out, heads_out, depth), jnp.bfloat16),
        in_specs=[pl.BlockSpec(memory_space=VMEM)] * 2,
        out_specs=pl.BlockSpec(memory_space=VMEM),
        compiler_params=pltpu.CompilerParams(vmem_limit_bytes=16 * MIB),
        name="settle",
    )(main, stats)


def project(own_share, rows, early, wo, n_block, tiles, spot):
    n_all, heads_here, _ = rows.shape
    n_early, depth, piece = early.shape
    n_late = n_block - n_early
    n_rows = n_all // len(tiles)

    def body(own_ref, x_ref, early_ref, wo_ref, out_ref, late, wide, packed, sem):
        fetch = weight_fetch(wo_ref, late, sem, own_ref[0], n_block, piece)
        fetch_wo = [fetch(n_early + b, b) for b in range(n_late)]
        for copy in fetch_wo:
            copy.start()

        @pl.when(own_ref[0] >= 0)
        def _():
            wide[...] = x_ref[...].astype(jnp.float32).reshape(n_all * heads_here, HD)
            for j in range(heads_here):
                pieces = [
                    wide[pl.ds(first * heads_here + j, n_rows, stride=heads_here * step), :]
                    for first, step in tiles
                ]
                packed[:, HD * j : HD * (j + 1)] = jnp.concatenate(pieces, axis=0).astype(jnp.bfloat16)
            x = packed[...]
            for b in range(n_block):
                if b < n_early:
                    block = early_ref[b]
                else:
                    fetch_wo[b - n_early].wait()
                    block = late[b - n_early]
                share = jnp.dot(x, block, preferred_element_type=jnp.float32)
                for s in range(len(tiles)):
                    out_ref[spot(b, s)] = share[s * n_rows : (s + 1) * n_rows].astype(jnp.bfloat16)

    in_vmem = pl.BlockSpec(memory_space=VMEM)
    return pl.pallas_call(
        body,
        out_shape=jax.ShapeDtypeStruct((n_block * len(tiles), n_rows, piece), jnp.bfloat16),
        in_specs=[
            pl.BlockSpec(memory_space=SMEM), in_vmem, in_vmem, pl.BlockSpec(memory_space=HBM)
        ],
        out_specs=in_vmem,
        scratch_shapes=[
            pltpu.VMEM((n_late, depth, piece), wo.dtype),
            pltpu.VMEM((n_all * heads_here, HD), jnp.float32),
            pltpu.VMEM((n_all, heads_here * HD), jnp.bfloat16),
            pltpu.SemaphoreType.DMA((n_late,)),
        ],
        compiler_params=pltpu.CompilerParams(vmem_limit_bytes=24 * MIB),
        name="project",
    )(own_share, rows, early, in_place(wo))


def finish(shares, scales, residual, n_head, n_share, spot):
    piece = shares.shape[2]

    def body(share_ref, scale_ref, res_ref, out_ref):
        for s in range(n_share):
            total = share_ref[spot(0, s)].astype(jnp.float32)
            for h in range(1, n_head):
                total = total + share_ref[spot(h, s)].astype(jnp.float32)
            cols = slice(s * piece, (s + 1) * piece)
            out_ref[:, cols] = (
                res_ref[:, cols].astype(jnp.float32) + total * scale_ref[:, cols]
            ).astype(jnp.bfloat16)

    return pl.pallas_call(
        body,
        out_shape=jax.ShapeDtypeStruct(residual.shape, jnp.bfloat16),
        in_specs=[pl.BlockSpec(memory_space=VMEM)] * 3,
        out_specs=pl.BlockSpec(memory_space=VMEM),
        compiler_params=pltpu.CompilerParams(vmem_limit_bytes=16 * MIB),
        name="finish",
    )(shares, scales, residual)


def exchange(block, axes):
    return lax.all_to_all(block, axes, split_axis=0, concat_axis=0, tiled=True)


def on_device(
    queries, new_kv, positions, lengths, kv_codes, kv_scales, wo_codes, wo_scales, residual
):
    n_head = lax.axis_size("head")
    n_dp = lax.axis_size("dp")
    my_head = lax.axis_index("head")
    n_rows, width = queries.shape
    heads_here = width // HD
    n_heads = heads_here * n_head
    n_kv = new_kv.shape[2] // HD
    block_len = kv_codes.shape[2]
    own_cols = wo_codes.shape[1] // n_head
    n_group = lax.axis_size("group")
    if own_cols % (n_group * n_dp * 128):
        n_group = 1
    n_share = n_group * n_dp
    piece = own_cols // n_share
    my_share = lax.axis_index("dp")
    axes = ("head", "dp")
    if n_group > 1:
        my_share = my_share + n_dp * lax.axis_index("group")
        axes = ("group", "head", "dp")

    def spot(head, share):
        return (share // n_dp * n_head + head) * n_dp + share % n_dp

    gathered = exchange(jnp.broadcast_to(queries, (n_head, n_rows, width)), "head")
    cosine, sine = rotary_tables(positions)
    spread = jnp.repeat(jnp.swapaxes(kv_scales, 2, 3), n_heads // n_kv, axis=3)
    own_share = my_share.reshape(1).astype(jnp.int32)
    first_slot = (my_head * block_len).reshape(1).astype(jnp.int32)
    scalars = jnp.concatenate([lengths, first_slot, own_share])
    new_staged, kv_staged = stage((new_kv, kv_codes))
    partial, early = attend(
        scalars, gathered, cosine, sine, new_staged, kv_staged, spread[:, 0], spread[:, 1], wo_codes,
        EARLY_EIGHTHS * n_head // 8, piece,
    )
    own_share, partial = lax.optimization_barrier((own_share, partial))

    cuts = max(1, n_head // n_rows)
    depth = HD // cuts
    if cuts == 1:
        main = exchange(partial, "head")
        stats, stat_row = main, n_heads
    else:
        values = partial[:, :n_heads].reshape(n_rows, n_heads, cuts, depth).swapaxes(1, 2)
        stats = partial[:, n_heads:].reshape(n_rows, 1, STAT_ROWS * cuts, depth)
        stats = jnp.broadcast_to(stats, (n_rows, cuts) + stats.shape[2:])
        message = jnp.concatenate([values, stats], axis=2)
        received = exchange(message.reshape((n_head,) + message.shape[2:]), "head")
        main, stat_row = received[:, :n_heads], 0
        stats = received[:, n_heads:].reshape(n_head, STAT_ROWS, HD)
    copies = settle(
        main, stats, n_heads, stat_row, n_head, lambda h: [spot(h, s) for s in range(n_share)]
    )
    rows = exchange(copies, axes)
    if cuts > 1:
        rows = rows.reshape(n_group, n_rows, cuts, n_dp, heads_here, depth)
        rows = rows.transpose(0, 1, 3, 4, 2, 5).reshape(n_rows * n_share, heads_here, HD)
    tiles = [(s // n_dp * n_rows * n_dp + s % n_dp, n_dp) for s in range(n_share)]
    shares = exchange(project(own_share, rows, early, wo_codes, n_head, tiles, spot), axes)
    return finish(shares, wo_scales.reshape(1, own_cols), residual, n_head, n_share, spot)


def solution(mesh):
    placed = (
        P(("group", "dp"), "head"),
        P(("group", "dp"), None, None),
        P(("group", "dp")),
        P(("group", "dp")),
        P(("group", "dp"), None, "head", None),
        P(("group", "dp"), None, None, "head"),
        P("head", None),
        P("head"),
        P(("group", "dp"), "head"),
    )
    return jax.shard_map(
        on_device, mesh=mesh, in_specs=placed, out_specs=P(("group", "dp"), "head"), check_vma=False
    )
```

```python
import functools
import jax
import jax.numpy as jnp
from jax import lax
from jax.experimental import pallas as pl
from jax.experimental.pallas import tpu as pltpu
from jax.sharding import PartitionSpec as P


HD = 128
ROPE_BASE = 500000.0
NEG_FILL = -1e30
STAT_ROWS = 8
SIDE_ROWS = 8
ROW_UNROLL = 2
EARLY_EIGHTHS = 3
MIB = 1 << 20
VMEM = pltpu.MemorySpace.VMEM
SMEM = pltpu.MemorySpace.SMEM
HBM = pltpu.MemorySpace.HBM


def split3(value):
    high = value.astype(jnp.bfloat16)
    rest = value - high.astype(jnp.float32)
    middle = rest.astype(jnp.bfloat16)
    low = (rest - middle.astype(jnp.float32)).astype(jnp.bfloat16)
    return high, middle, low


def contract(left, right, dims):
    return lax.dot_general(left, right, (dims, ((), ())), preferred_element_type=jnp.float32)


def in_place(array):
    return pltpu.with_memory_space_constraint(array, HBM)


def rotary_tables(positions):
    half_dim = HD // 2
    inverse_rate = ROPE_BASE ** (-(jnp.arange(half_dim, dtype=jnp.float32) * (2.0 / HD)))
    angles = positions.astype(jnp.float32)[:, None] * inverse_rate
    cosine = jnp.cos(angles)
    sine = jnp.sin(angles)
    return jnp.concatenate([cosine, cosine], -1), jnp.concatenate([-sine, sine], -1)


def prepare(own_half, queries, kv_codes, kv_scales, count):
    half = queries.shape[0] // 2
    width = queries.shape[1]

    def body(own_ref, q_hbm, kv_hbm, sc_hbm, out_ref, k_ref, v_ref, sc_ref, whole, parts, sem):
        other = (1 - own_ref[0]) * half
        loads = [
            pltpu.make_async_copy(q_hbm, whole, sem.at[0]),
            pltpu.make_async_copy(kv_hbm.at[pl.ds(other, half), 0], k_ref, sem.at[1]),
            pltpu.make_async_copy(kv_hbm.at[pl.ds(other, half), 1], v_ref, sem.at[2]),
            pltpu.make_async_copy(sc_hbm.at[pl.ds(other, half)], sc_ref, sem.at[3]),
        ]
        for copy in loads:
            copy.start()
        loads[0].wait()
        for p in range(2):
            parts[p] = whole[p * half : (p + 1) * half, :]
        sends = [
            pltpu.make_async_copy(parts.at[n % 2], out_ref.at[n], sem.at[4 + n])
            for n in range(count)
        ]
        for copy in sends:
            copy.start()
        for copy in loads[1:] + sends:
            copy.wait()

    in_hbm, in_vmem = pl.BlockSpec(memory_space=HBM), pl.BlockSpec(memory_space=VMEM)
    return pl.pallas_call(
        body,
        out_shape=(
            pltpu.HBM((count, half, width), queries.dtype),
            pltpu.VMEM((half,) + kv_codes.shape[2:], kv_codes.dtype),
            pltpu.VMEM((half,) + kv_codes.shape[2:], kv_codes.dtype),
            pltpu.VMEM((half,) + kv_scales.shape[1:], kv_scales.dtype),
        ),
        in_specs=[pl.BlockSpec(memory_space=SMEM)] + [in_hbm] * 3,
        out_specs=(in_hbm, in_vmem, in_vmem, in_vmem),
        scratch_shapes=[
            pltpu.VMEM(queries.shape, queries.dtype),
            pltpu.VMEM((2, half, width), queries.dtype),
            pltpu.SemaphoreType.DMA((4 + count,)),
        ],
        compiler_params=pltpu.CompilerParams(vmem_limit_bytes=MIB // 2),
        name="prepare",
    )(own_half, in_place(queries), in_place(kv_codes), in_place(kv_scales))


def stage(own_half, arrays):
    half = arrays[0].shape[0] // 2
    count = len(arrays)

    def body(own_ref, *refs):
        first = own_ref[0] * half
        copies = [
            pltpu.make_async_copy(refs[n].at[pl.ds(first, half)], refs[count + n], refs[-1].at[n])
            for n in range(count)
        ]
        for copy in copies:
            copy.start()
        for copy in copies:
            copy.wait()

    in_hbm, in_vmem = pl.BlockSpec(memory_space=HBM), pl.BlockSpec(memory_space=VMEM)
    return pl.pallas_call(
        body,
        out_shape=tuple(pltpu.VMEM((half,) + a.shape[1:], a.dtype) for a in arrays),
        in_specs=[pl.BlockSpec(memory_space=SMEM)] + [in_hbm] * count,
        out_specs=(in_vmem,) * count,
        scratch_shapes=[pltpu.SemaphoreType.DMA((count,))],
        compiler_params=pltpu.CompilerParams(vmem_limit_bytes=MIB // 4),
        name="stage",
    )(own_half, *[in_place(a) for a in arrays])


def weight_fetch(wo_ref, out_ref, sem, share, n_block, piece):
    def fetch(block, slot):
        start = block * (wo_ref.shape[1] // n_block) + share * piece
        cols = pl.ds(pl.multiple_of(start, 128), piece)
        return pltpu.make_async_copy(wo_ref.at[:, cols], out_ref.at[slot], sem.at[slot])

    return fetch


def score(
    scalars, gathered, cosine, sine, new_kv, own_kv, other_keys, own_scales, other_scales, wo,
    n_early, piece,
):
    n_src, n_rows, width = gathered.shape
    heads_here = width // HD
    n_heads = n_src * heads_here
    block_len = own_kv.shape[2]
    n_kv = own_kv.shape[3] // HD
    group = n_heads // n_kv
    score_scale = HD ** (-0.5)

    def body(
        s_ref, q_ref, cos_ref, sin_ref, new_ref, own_ref, other_ref, own_sc, other_sc, wo_ref,
        weight_ref, side_ref, early_ref, qs, ks, wo_sem,
    ):
        fetch = weight_fetch(wo_ref, early_ref, wo_sem, s_ref[n_rows + 3], n_src, piece)
        fetch_wo = [fetch(b, b) for b in range(n_early)]
        for copy in fetch_wo:
            copy.start()
        cos, sin = cos_ref[...], sin_ref[...]

        def rotate(tile):
            return tile * cos + pltpu.roll(tile, HD // 2, 1) * sin

        for src in range(n_src):
            block = q_ref[src].astype(jnp.float32)
            for j in range(heads_here):
                head = src * heads_here + j
                qs[n_rows * head : n_rows * (head + 1), :] = rotate(block[:, HD * j : HD * (j + 1)])
        fresh = new_ref[:, 0, :].astype(jnp.float32)
        for k in range(n_kv):
            ks[n_rows * k : n_rows * (k + 1), :] = rotate(fresh[:, HD * k : HD * (k + 1)])

        is_first = s_ref[n_rows + 2] == 0
        lane_group = lax.broadcasted_iota(jnp.int32, (1, n_heads), 1) // group
        place = lax.broadcasted_iota(jnp.int32, (block_len, n_heads), 0)
        slot = jnp.concatenate([s_ref[n_rows] + place, s_ref[n_rows + 1] + place], axis=0)
        owner = lax.broadcasted_iota(jnp.int32, (n_kv, n_heads), 0) == lane_group
        one_hot = owner.astype(jnp.float32)
        both = ((0,), (0,))

        def spread(kind, r):
            parts = [
                lax.dot_general(
                    ref[r, kind], one_hot, (both, ((), ())), precision=lax.Precision.HIGHEST,
                    preferred_element_type=jnp.float32,
                )
                for ref in (own_sc, other_sc)
            ]
            return jnp.concatenate(parts, axis=0)

        def keys_of(r):
            parts = [own_ref[r, 0, :, HD * k : HD * (k + 1)] for k in range(n_kv)]
            parts += [other_ref[r, :, HD * k : HD * (k + 1)] for k in range(n_kv)]
            return jnp.concatenate(parts, axis=0)

        def one_row(r):
            query = qs[pl.ds(r, n_heads, stride=n_rows), :].astype(jnp.bfloat16)
            raw = contract(keys_of(r), query, ((1,), (1,)))
            halves = []
            for base in (0, n_kv):
                picked = jnp.zeros((block_len, n_heads), jnp.float32)
                for k in range(n_kv):
                    first = block_len * (base + k)
                    picked = jnp.where(lane_group == k, raw[first : first + block_len], picked)
                halves.append(picked)
            raw_own = jnp.concatenate(halves, axis=0)
            is_valid = slot < s_ref[r]
            scores = jnp.where(is_valid, raw_own * spread(0, r) * score_scale, NEG_FILL)
            fresh_key = ks[pl.ds(r, n_kv, stride=n_rows), :].astype(jnp.bfloat16)
            fresh_raw = contract(fresh_key, query, ((1,), (1,)))
            fresh_score = jnp.sum(jnp.where(owner, fresh_raw, 0.0), axis=0, keepdims=True) * score_scale
            fresh_score = jnp.where(is_first, fresh_score, NEG_FILL)
            peak = jnp.maximum(jnp.max(scores, axis=0, keepdims=True), fresh_score)
            weights = jnp.where(is_valid, jnp.exp(scores - peak), 0.0)
            fresh_weight = jnp.where(is_first, jnp.exp(fresh_score - peak), 0.0)
            total = jnp.sum(weights, axis=0, keepdims=True) + fresh_weight
            weight_ref[r] = weights * spread(1, r)
            pad = jnp.zeros((SIDE_ROWS - 3, n_heads), jnp.float32)
            side_ref[r] = jnp.concatenate([peak, total, fresh_weight, pad], axis=0)

        def some_rows(step, carry):
            for u in range(ROW_UNROLL):
                one_row(step * ROW_UNROLL + u)
            return carry

        lax.fori_loop(0, n_rows // ROW_UNROLL, some_rows, 0)
        for copy in fetch_wo:
            copy.wait()

    in_vmem = pl.BlockSpec(memory_space=VMEM)
    return pl.pallas_call(
        body,
        out_shape=(
            pltpu.VMEM((n_rows, 2 * block_len, n_heads), jnp.float32),
            pltpu.VMEM((n_rows, SIDE_ROWS, n_heads), jnp.float32),
            pltpu.VMEM((n_early, wo.shape[0], piece), wo.dtype),
        ),
        in_specs=[pl.BlockSpec(memory_space=SMEM)]
        + [in_vmem] * 8 + [pl.BlockSpec(memory_space=HBM)],
        out_specs=(in_vmem,) * 3,
        scratch_shapes=[
            pltpu.VMEM((n_rows * n_heads, HD), jnp.float32),
            pltpu.VMEM((n_rows * n_kv, HD), jnp.float32),
            pltpu.SemaphoreType.DMA((n_early,)),
        ],
        compiler_params=pltpu.CompilerParams(vmem_limit_bytes=6 * MIB),
        name="score",
    )(
        scalars, gathered, cosine, sine, new_kv, own_kv, other_keys, own_scales, other_scales,
        in_place(wo),
    )


def blend(weights, side, new_kv, own_kv, other_values):
    n_rows, _, n_heads = weights.shape
    block_len = own_kv.shape[2]
    n_kv = own_kv.shape[3] // HD
    group = n_heads // n_kv

    def body(weight_ref, side_ref, new_ref, own_ref, other_ref, out_ref):
        lane_group = lax.broadcasted_iota(jnp.int32, (1, n_heads), 1) // group
        owner = lax.broadcasted_iota(jnp.int32, (n_kv, n_heads), 0) == lane_group
        both = ((0,), (0,))

        def one_row(r):
            scaled = weight_ref[r]
            wide = jnp.concatenate(
                [
                    jnp.where(lane_group == k, scaled[first : first + block_len], 0.0)
                    for first in (0, block_len)
                    for k in range(n_kv)
                ],
                axis=0,
            )
            high = wide.astype(jnp.bfloat16)
            low = (wide - high.astype(jnp.float32)).astype(jnp.bfloat16)
            peak, total, fresh_weight = side_ref[r, 0:1], side_ref[r, 1:2], side_ref[r, 2:3]
            fresh_spread = jnp.where(owner, fresh_weight, 0.0)
            fresh_high = fresh_spread.astype(jnp.bfloat16)
            fresh_low = (fresh_spread - fresh_high.astype(jnp.float32)).astype(jnp.bfloat16)
            fresh_value = jnp.concatenate(
                [new_ref[pl.ds(r, 1), 1, HD * k : HD * (k + 1)] for k in range(n_kv)], axis=0
            )
            values = [own_ref[r, 1, :, HD * k : HD * (k + 1)] for k in range(n_kv)]
            values += [other_ref[r, :, HD * k : HD * (k + 1)] for k in range(n_kv)]
            values = jnp.concatenate(values, axis=0)
            summed = contract(high, values, both) + contract(low, values, both)
            summed = summed + (
                contract(fresh_high, fresh_value, both) + contract(fresh_low, fresh_value, both)
            )
            out_ref[r, 0:n_heads, :] = summed.astype(jnp.bfloat16)
            parts = split3(peak) + split3(total)
            pad = jnp.zeros((STAT_ROWS - len(parts), n_heads), jnp.float32)
            stats = jnp.concatenate([part.astype(jnp.float32) for part in parts] + [pad], axis=0)
            out_ref[r, n_heads : n_heads + STAT_ROWS, :] = stats.astype(jnp.bfloat16)

        for r in range(n_rows):
            one_row(r)

    return pl.pallas_call(
        body,
        out_shape=jax.ShapeDtypeStruct((n_rows, n_heads + STAT_ROWS, HD), jnp.bfloat16),
        in_specs=[pl.BlockSpec(memory_space=VMEM)] * 5,
        out_specs=pl.BlockSpec(memory_space=VMEM),
        compiler_params=pltpu.CompilerParams(vmem_limit_bytes=6 * MIB),
        name="blend",
    )(weights, side, new_kv, own_kv, other_values)


def settle(main, stats, n_heads, stat_row, n_target, copies):
    n_src = main.shape[0]
    depth = main.shape[2]
    heads_root = n_heads ** (-0.5)
    heads_out = n_heads // n_target
    n_out = n_target * len(copies(0))

    def body(main_ref, stat_ref, out_ref):
        peaks, totals = [], []
        for b in range(n_src):
            part = stat_ref[b, stat_row : stat_row + STAT_ROWS, :].astype(jnp.float32)
            peaks.append(part[0:1] + part[1:2] + part[2:3])
            totals.append(part[3:4] + part[4:5] + part[5:6])
        peak = functools.reduce(jnp.maximum, peaks)
        scales = [jnp.exp(p - peak) for p in peaks]
        total = functools.reduce(jnp.add, [s * t for s, t in zip(scales, totals)])
        common = lax.broadcasted_iota(jnp.int32, (n_heads, n_heads), 0) & lax.broadcasted_iota(
            jnp.int32, (n_heads, n_heads), 1
        )
        bits = (n_heads - 1).bit_length()
        parity = common
        for bit in range(1, bits):
            parity = parity ^ (common >> bit)
        sign = jnp.where((parity & 1) == 0, heads_root, -heads_root)
        acc = jnp.zeros((n_heads, depth), jnp.float32)
        for b in range(n_src):
            mixed = sign * (scales[b] / total)
            high = mixed.astype(jnp.bfloat16)
            low = (mixed - high.astype(jnp.float32)).astype(jnp.bfloat16)
            value = main_ref[b, 0:n_heads, :]
            acc = acc + jnp.dot(high, value, preferred_element_type=jnp.float32)
            acc = acc + jnp.dot(low, value, preferred_element_type=jnp.float32)
        rotated = acc.astype(jnp.bfloat16)
        for h in range(n_target):
            for spot in copies(h):
                out_ref[spot] = rotated[h * heads_out : (h + 1) * heads_out]

    return pl.pallas_call(
        body,
        out_shape=jax.ShapeDtypeStruct((n_out, heads_out, depth), jnp.bfloat16),
        in_specs=[pl.BlockSpec(memory_space=VMEM)] * 2,
        out_specs=pl.BlockSpec(memory_space=VMEM),
        compiler_params=pltpu.CompilerParams(vmem_limit_bytes=16 * MIB),
        name="settle",
    )(main, stats)


def project(own_share, rows, early, wo, n_block, tiles, spot):
    n_all, heads_here, _ = rows.shape
    n_early, depth, piece = early.shape
    n_late = n_block - n_early
    n_rows = n_all // len(tiles)

    def body(own_ref, x_ref, early_ref, wo_ref, out_ref, late, wide, packed, sem):
        fetch = weight_fetch(wo_ref, late, sem, own_ref[0], n_block, piece)
        fetch_wo = [fetch(n_early + b, b) for b in range(n_late)]
        for copy in fetch_wo:
            copy.start()

        @pl.when(own_ref[0] >= 0)
        def _():
            wide[...] = x_ref[...].astype(jnp.float32).reshape(n_all * heads_here, HD)
            for j in range(heads_here):
                pieces = [
                    wide[pl.ds(first * heads_here + j, n_rows, stride=heads_here * step), :]
                    for first, step in tiles
                ]
                packed[:, HD * j : HD * (j + 1)] = jnp.concatenate(pieces, axis=0).astype(jnp.bfloat16)
            x = packed[...]
            for b in range(n_block):
                if b < n_early:
                    block = early_ref[b]
                else:
                    fetch_wo[b - n_early].wait()
                    block = late[b - n_early]
                share = jnp.dot(x, block, preferred_element_type=jnp.float32)
                for s in range(len(tiles)):
                    out_ref[spot(b, s)] = share[s * n_rows : (s + 1) * n_rows].astype(jnp.bfloat16)

    in_vmem = pl.BlockSpec(memory_space=VMEM)
    return pl.pallas_call(
        body,
        out_shape=jax.ShapeDtypeStruct((n_block * len(tiles), n_rows, piece), jnp.bfloat16),
        in_specs=[
            pl.BlockSpec(memory_space=SMEM), in_vmem, in_vmem, pl.BlockSpec(memory_space=HBM)
        ],
        out_specs=in_vmem,
        scratch_shapes=[
            pltpu.VMEM((n_late, depth, piece), wo.dtype),
            pltpu.VMEM((n_all * heads_here, HD), jnp.float32),
            pltpu.VMEM((n_all, heads_here * HD), jnp.bfloat16),
            pltpu.SemaphoreType.DMA((n_late,)),
        ],
        compiler_params=pltpu.CompilerParams(vmem_limit_bytes=24 * MIB),
        name="project",
    )(own_share, rows, early, in_place(wo))


def finish(shares, scales, residual, n_head, n_share, spot):
    piece = shares.shape[2]

    n_rows = shares.shape[1]

    def body(share_ref, scale_ref, res_ref, out_ref, held):
        for s in range(n_share):
            total = share_ref[spot(0, s)].astype(jnp.float32)
            for h in range(1, n_head):
                total = total + share_ref[spot(h, s)].astype(jnp.float32)
            for c in range(piece // HD):
                held[s * (piece // HD) + c] = total[:, HD * c : HD * (c + 1)]
        for c in range(n_share * piece // HD):
            cols = slice(HD * c, HD * (c + 1))
            ordered = [held[c, pl.ds(p, n_rows // 2, stride=2), :] for p in range(2)]
            total = jnp.concatenate(ordered, axis=0)
            out_ref[:, cols] = (
                res_ref[:, cols].astype(jnp.float32) + total * scale_ref[:, cols]
            ).astype(jnp.bfloat16)

    return pl.pallas_call(
        body,
        out_shape=jax.ShapeDtypeStruct(residual.shape, jnp.bfloat16),
        in_specs=[pl.BlockSpec(memory_space=VMEM)] * 3,
        out_specs=pl.BlockSpec(memory_space=VMEM),
        scratch_shapes=[pltpu.VMEM((n_share * piece // HD, n_rows, HD), jnp.float32)],
        compiler_params=pltpu.CompilerParams(vmem_limit_bytes=16 * MIB),
        name="finish",
    )(shares, scales, residual)


def exchange(block, axes, groups=None):
    return lax.all_to_all(
        block, axes, split_axis=0, concat_axis=0, tiled=True, axis_index_groups=groups
    )


def on_device(
    queries, new_kv, positions, lengths, kv_codes, kv_scales, wo_codes, wo_scales, residual
):
    n_head = lax.axis_size("head")
    n_dp = lax.axis_size("dp")
    my_head = lax.axis_index("head")
    n_rows, width = queries.shape
    heads_here = width // HD
    n_heads = heads_here * n_head
    block_len = kv_codes.shape[2]
    own_cols = wo_codes.shape[1] // n_head
    n_group = lax.axis_size("group")
    if own_cols % (n_group * n_dp * 128):
        n_group = 1
    n_share = n_group * n_dp
    piece = own_cols // n_share
    my_share = lax.axis_index("dp")
    axes = ("head", "dp")
    if n_group > 1:
        my_share = my_share + n_dp * lax.axis_index("group")
        axes = ("group", "head", "dp")

    def spot(head, share):
        return (share // n_dp * n_head + head) * n_dp + share % n_dp

    half = n_rows // 2
    n_line = n_head // 2
    my_line = my_head // 2
    parity = (my_head % 2).astype(jnp.int32)
    pairs = [(i, i ^ 1) for i in range(n_head)]
    lines = [list(range(p, n_head, 2)) for p in range(2)]

    def rows_of(array, side):
        return lax.dynamic_slice_in_dim(array, side * half, half, axis=0)

    own_half = parity.reshape(1)
    messages, keys_out, values_out, scales_out = prepare(
        own_half, queries, kv_codes, kv_scales, n_head
    )
    other_keys = lax.ppermute(keys_out, "head", pairs)
    other_scales = lax.ppermute(scales_out, "head", pairs)
    gathered = exchange(messages, "head")
    other_values = lax.ppermute(values_out, "head", pairs)
    cosine, sine = rotary_tables(rows_of(positions, parity))
    own_share = my_share.reshape(1).astype(jnp.int32)
    slots = [my_head * block_len, (my_head ^ 1) * block_len, my_line]
    slots = jnp.stack(slots).astype(jnp.int32)
    scalars = jnp.concatenate([rows_of(lengths, parity), slots, own_share])
    new_staged, kv_staged, scales_staged = stage(
        own_half, (new_kv, kv_codes, kv_scales)
    )
    weights, side, early = score(
        scalars, gathered, cosine, sine, new_staged, kv_staged, other_keys, scales_staged,
        other_scales, wo_codes, EARLY_EIGHTHS * n_head // 8, piece,
    )
    partial = blend(weights, side, new_staged, kv_staged, other_values)
    own_share, partial = lax.optimization_barrier((own_share, partial))

    cuts = max(1, n_line // half)
    depth = HD // cuts
    if cuts == 1:
        main = exchange(partial, "head", lines)
        stats, stat_row = main, n_heads
    else:
        values = partial[:, :n_heads].reshape(half, n_heads, cuts, depth).swapaxes(1, 2)
        stats = partial[:, n_heads:].reshape(half, 1, STAT_ROWS * cuts, depth)
        stats = jnp.broadcast_to(stats, (half, cuts) + stats.shape[2:])
        message = jnp.concatenate([values, stats], axis=2)
        received = exchange(message.reshape((n_line,) + message.shape[2:]), "head", lines)
        main, stat_row = received[:, :n_heads], 0
        stats = received[:, n_heads:].reshape(n_line, STAT_ROWS, HD)
    copies = settle(
        main, stats, n_heads, stat_row, n_head, lambda h: [spot(h, s) for s in range(n_share)]
    )
    rows = exchange(copies, axes)
    if cuts > 1:
        rows = rows.reshape(n_group, half, cuts, 2, n_dp, heads_here, depth)
        rows = rows.transpose(0, 1, 3, 4, 5, 2, 6).reshape(n_rows * n_share, heads_here, HD)
    tiles = [(s // n_dp * n_rows * n_dp + s % n_dp, n_dp) for s in range(n_share)]
    shares = exchange(project(own_share, rows, early, wo_codes, n_head, tiles, spot), axes)
    return finish(shares, wo_scales.reshape(1, own_cols), residual, n_head, n_share, spot)


def solution(mesh):
    placed = (
        P(("group", "dp"), "head"),
        P(("group", "dp"), None, None),
        P(("group", "dp")),
        P(("group", "dp")),
        P(("group", "dp"), None, "head", None),
        P(("group", "dp"), None, None, "head"),
        P("head", None),
        P("head"),
        P(("group", "dp"), "head"),
    )
    return jax.shard_map(
        on_device, mesh=mesh, in_specs=placed, out_specs=P(("group", "dp"), "head"), check_vma=False
    )
```

```python
import functools
import jax
import jax.numpy as jnp
from jax import lax
from jax.experimental import pallas as pl
from jax.experimental.pallas import tpu as pltpu
from jax.sharding import PartitionSpec as P


HD = 128
ROPE_BASE = 500000.0
NEG_FILL = -1e30
STAT_ROWS = 8
SIDE_ROWS = 8
ROW_UNROLL = 2
EARLY_EIGHTHS = 5
MIB = 1 << 20
VMEM = pltpu.MemorySpace.VMEM
SMEM = pltpu.MemorySpace.SMEM
HBM = pltpu.MemorySpace.HBM


def split3(value):
    high = value.astype(jnp.bfloat16)
    rest = value - high.astype(jnp.float32)
    middle = rest.astype(jnp.bfloat16)
    low = (rest - middle.astype(jnp.float32)).astype(jnp.bfloat16)
    return high, middle, low


def contract(left, right, dims):
    return lax.dot_general(left, right, (dims, ((), ())), preferred_element_type=jnp.float32)


def in_place(array):
    return pltpu.with_memory_space_constraint(array, HBM)


def rotary_tables(positions):
    half_dim = HD // 2
    inverse_rate = ROPE_BASE ** (-(jnp.arange(half_dim, dtype=jnp.float32) * (2.0 / HD)))
    angles = positions.astype(jnp.float32)[:, None] * inverse_rate
    cosine = jnp.cos(angles)
    sine = jnp.sin(angles)
    return jnp.concatenate([cosine, cosine], -1), jnp.concatenate([-sine, sine], -1)


def prepare(own_half, queries, kv_codes, kv_scales, count):
    half = queries.shape[0] // 2
    width = queries.shape[1]

    def body(own_ref, q_hbm, kv_hbm, sc_hbm, out_ref, k_ref, v_ref, sc_ref, whole, parts, sem):
        other = (1 - own_ref[0]) * half
        loads = [
            pltpu.make_async_copy(q_hbm, whole, sem.at[0]),
            pltpu.make_async_copy(kv_hbm.at[pl.ds(other, half), 0], k_ref, sem.at[1]),
            pltpu.make_async_copy(kv_hbm.at[pl.ds(other, half), 1], v_ref, sem.at[2]),
            pltpu.make_async_copy(sc_hbm.at[pl.ds(other, half)], sc_ref, sem.at[3]),
        ]
        for copy in loads:
            copy.start()
        loads[0].wait()
        for p in range(2):
            parts[p] = whole[p * half : (p + 1) * half, :]
        sends = [
            pltpu.make_async_copy(parts.at[n % 2], out_ref.at[n], sem.at[4 + n])
            for n in range(count)
        ]
        for copy in sends:
            copy.start()
        for copy in loads[1:] + sends:
            copy.wait()

    in_hbm, in_vmem = pl.BlockSpec(memory_space=HBM), pl.BlockSpec(memory_space=VMEM)
    return pl.pallas_call(
        body,
        out_shape=(
            pltpu.HBM((count, half, width), queries.dtype),
            pltpu.VMEM((half,) + kv_codes.shape[2:], kv_codes.dtype),
            pltpu.VMEM((half,) + kv_codes.shape[2:], kv_codes.dtype),
            pltpu.VMEM((half,) + kv_scales.shape[1:], kv_scales.dtype),
        ),
        in_specs=[pl.BlockSpec(memory_space=SMEM)] + [in_hbm] * 3,
        out_specs=(in_hbm, in_vmem, in_vmem, in_vmem),
        scratch_shapes=[
            pltpu.VMEM(queries.shape, queries.dtype),
            pltpu.VMEM((2, half, width), queries.dtype),
            pltpu.SemaphoreType.DMA((4 + count,)),
        ],
        compiler_params=pltpu.CompilerParams(vmem_limit_bytes=MIB // 2),
        name="prepare",
    )(own_half, in_place(queries), in_place(kv_codes), in_place(kv_scales))


def stage(own_half, arrays):
    half = arrays[0].shape[0] // 2
    count = len(arrays)

    def body(own_ref, *refs):
        first = own_ref[0] * half
        copies = [
            pltpu.make_async_copy(refs[n].at[pl.ds(first, half)], refs[count + n], refs[-1].at[n])
            for n in range(count)
        ]
        for copy in copies:
            copy.start()
        for copy in copies:
            copy.wait()

    in_hbm, in_vmem = pl.BlockSpec(memory_space=HBM), pl.BlockSpec(memory_space=VMEM)
    return pl.pallas_call(
        body,
        out_shape=tuple(pltpu.VMEM((half,) + a.shape[1:], a.dtype) for a in arrays),
        in_specs=[pl.BlockSpec(memory_space=SMEM)] + [in_hbm] * count,
        out_specs=(in_vmem,) * count,
        scratch_shapes=[pltpu.SemaphoreType.DMA((count,))],
        compiler_params=pltpu.CompilerParams(vmem_limit_bytes=MIB // 4),
        name="stage",
    )(own_half, *[in_place(a) for a in arrays])


def weight_fetch(wo_ref, out_ref, sem, share, n_block, piece):
    def fetch(block, slot):
        start = block * (wo_ref.shape[1] // n_block) + share * piece
        cols = pl.ds(pl.multiple_of(start, 128), piece)
        return pltpu.make_async_copy(wo_ref.at[:, cols], out_ref.at[slot], sem.at[slot])

    return fetch


def score(
    facts, gathered, cosine, sine, new_kv, own_kv, other_keys, own_scales, other_scales, wo,
    n_early, piece,
):
    n_src, n_rows, width = gathered.shape
    heads_here = width // HD
    n_heads = n_src * heads_here
    block_len = own_kv.shape[2]
    n_kv = own_kv.shape[3] // HD
    group = n_heads // n_kv
    score_scale = HD ** (-0.5)

    def body(
        fact_ref, q_ref, cos_ref, sin_ref, new_ref, own_ref, other_ref, own_sc, other_sc, wo_ref,
        weight_ref, side_ref, early_ref, qs, ks, wo_sem,
    ):
        fetch = weight_fetch(wo_ref, early_ref, wo_sem, fact_ref[2 * n_rows + 4], n_src, piece)
        fetch_wo = [fetch(b, b) for b in range(n_early)]
        for copy in fetch_wo:
            copy.start()
        first_row = fact_ref[2 * n_rows]
        cos, sin = [
            jnp.where(first_row == 0, ref[:n_rows], ref[n_rows:]) for ref in (cos_ref, sin_ref)
        ]

        def rotate(tile):
            return tile * cos + pltpu.roll(tile, HD // 2, 1) * sin

        for src in range(n_src):
            block = q_ref[src].astype(jnp.float32)
            for j in range(heads_here):
                head = src * heads_here + j
                qs[n_rows * head : n_rows * (head + 1), :] = rotate(block[:, HD * j : HD * (j + 1)])
        fresh = new_ref[:, 0, :].astype(jnp.float32)
        for k in range(n_kv):
            ks[n_rows * k : n_rows * (k + 1), :] = rotate(fresh[:, HD * k : HD * (k + 1)])

        is_first = fact_ref[2 * n_rows + 3] == 0
        lane_group = lax.broadcasted_iota(jnp.int32, (1, n_heads), 1) // group
        place = lax.broadcasted_iota(jnp.int32, (block_len, n_heads), 0)
        slot = jnp.concatenate([fact_ref[2 * n_rows + 1] + place, fact_ref[2 * n_rows + 2] + place], axis=0)
        owner = lax.broadcasted_iota(jnp.int32, (n_kv, n_heads), 0) == lane_group
        one_hot = owner.astype(jnp.float32)
        both = ((0,), (0,))

        def spread(kind, r):
            parts = [
                lax.dot_general(
                    ref[r, kind], one_hot, (both, ((), ())), precision=lax.Precision.HIGHEST,
                    preferred_element_type=jnp.float32,
                )
                for ref in (own_sc, other_sc)
            ]
            return jnp.concatenate(parts, axis=0)

        def keys_of(r):
            parts = [own_ref[r, 0, :, HD * k : HD * (k + 1)] for k in range(n_kv)]
            parts += [other_ref[r, :, HD * k : HD * (k + 1)] for k in range(n_kv)]
            return jnp.concatenate(parts, axis=0)

        def one_row(r):
            query = qs[pl.ds(r, n_heads, stride=n_rows), :].astype(jnp.bfloat16)
            raw = contract(keys_of(r), query, ((1,), (1,)))
            halves = []
            for base in (0, n_kv):
                picked = jnp.zeros((block_len, n_heads), jnp.float32)
                for k in range(n_kv):
                    first = block_len * (base + k)
                    picked = jnp.where(lane_group == k, raw[first : first + block_len], picked)
                halves.append(picked)
            raw_own = jnp.concatenate(halves, axis=0)
            is_valid = slot < fact_ref[first_row + r]
            scores = jnp.where(is_valid, raw_own * spread(0, r) * score_scale, NEG_FILL)
            fresh_key = ks[pl.ds(r, n_kv, stride=n_rows), :].astype(jnp.bfloat16)
            fresh_raw = contract(fresh_key, query, ((1,), (1,)))
            fresh_score = jnp.sum(jnp.where(owner, fresh_raw, 0.0), axis=0, keepdims=True) * score_scale
            fresh_score = jnp.where(is_first, fresh_score, NEG_FILL)
            peak = jnp.maximum(jnp.max(scores, axis=0, keepdims=True), fresh_score)
            weights = jnp.where(is_valid, jnp.exp(scores - peak), 0.0)
            fresh_weight = jnp.where(is_first, jnp.exp(fresh_score - peak), 0.0)
            total = jnp.sum(weights, axis=0, keepdims=True) + fresh_weight
            weight_ref[r] = weights * spread(1, r)
            pad = jnp.zeros((SIDE_ROWS - 3, n_heads), jnp.float32)
            side_ref[r] = jnp.concatenate([peak, total, fresh_weight, pad], axis=0)

        def some_rows(step, carry):
            for u in range(ROW_UNROLL):
                one_row(step * ROW_UNROLL + u)
            return carry

        lax.fori_loop(0, n_rows // ROW_UNROLL, some_rows, 0)
        for copy in fetch_wo:
            copy.wait()

    in_vmem = pl.BlockSpec(memory_space=VMEM)
    return pl.pallas_call(
        body,
        out_shape=(
            pltpu.VMEM((n_rows, 2 * block_len, n_heads), jnp.float32),
            pltpu.VMEM((n_rows, SIDE_ROWS, n_heads), jnp.float32),
            pltpu.VMEM((n_early, wo.shape[0], piece), wo.dtype),
        ),
        in_specs=[pl.BlockSpec(memory_space=SMEM)]
        + [in_vmem] * 8 + [pl.BlockSpec(memory_space=HBM)],
        out_specs=(in_vmem,) * 3,
        scratch_shapes=[
            pltpu.VMEM((n_rows * n_heads, HD), jnp.float32),
            pltpu.VMEM((n_rows * n_kv, HD), jnp.float32),
            pltpu.SemaphoreType.DMA((n_early,)),
        ],
        compiler_params=pltpu.CompilerParams(vmem_limit_bytes=6 * MIB),
        name="score",
    )(
        facts, gathered, cosine, sine, new_kv, own_kv, other_keys, own_scales, other_scales,
        in_place(wo),
    )


def blend(weights, side, new_kv, own_kv, other_values):
    n_rows, _, n_heads = weights.shape
    block_len = own_kv.shape[2]
    n_kv = own_kv.shape[3] // HD
    group = n_heads // n_kv

    def body(weight_ref, side_ref, new_ref, own_ref, other_ref, out_ref):
        lane_group = lax.broadcasted_iota(jnp.int32, (1, n_heads), 1) // group
        owner = lax.broadcasted_iota(jnp.int32, (n_kv, n_heads), 0) == lane_group
        both = ((0,), (0,))

        def one_row(r):
            scaled = weight_ref[r]
            wide = jnp.concatenate(
                [
                    jnp.where(lane_group == k, scaled[first : first + block_len], 0.0)
                    for first in (0, block_len)
                    for k in range(n_kv)
                ],
                axis=0,
            )
            high = wide.astype(jnp.bfloat16)
            low = (wide - high.astype(jnp.float32)).astype(jnp.bfloat16)
            peak, total, fresh_weight = side_ref[r, 0:1], side_ref[r, 1:2], side_ref[r, 2:3]
            fresh_spread = jnp.where(owner, fresh_weight, 0.0)
            fresh_high = fresh_spread.astype(jnp.bfloat16)
            fresh_low = (fresh_spread - fresh_high.astype(jnp.float32)).astype(jnp.bfloat16)
            fresh_value = jnp.concatenate(
                [new_ref[pl.ds(r, 1), 1, HD * k : HD * (k + 1)] for k in range(n_kv)], axis=0
            )
            values = [own_ref[r, 1, :, HD * k : HD * (k + 1)] for k in range(n_kv)]
            values += [other_ref[r, :, HD * k : HD * (k + 1)] for k in range(n_kv)]
            values = jnp.concatenate(values, axis=0)
            summed = contract(high, values, both) + contract(low, values, both)
            summed = summed + (
                contract(fresh_high, fresh_value, both) + contract(fresh_low, fresh_value, both)
            )
            out_ref[r, 0:n_heads, :] = summed.astype(jnp.bfloat16)
            parts = split3(peak) + split3(total)
            pad = jnp.zeros((STAT_ROWS - len(parts), n_heads), jnp.float32)
            stats = jnp.concatenate([part.astype(jnp.float32) for part in parts] + [pad], axis=0)
            out_ref[r, n_heads : n_heads + STAT_ROWS, :] = stats.astype(jnp.bfloat16)

        for r in range(n_rows):
            one_row(r)

    return pl.pallas_call(
        body,
        out_shape=jax.ShapeDtypeStruct((n_rows, n_heads + STAT_ROWS, HD), jnp.bfloat16),
        in_specs=[pl.BlockSpec(memory_space=VMEM)] * 5,
        out_specs=pl.BlockSpec(memory_space=VMEM),
        compiler_params=pltpu.CompilerParams(vmem_limit_bytes=6 * MIB),
        name="blend",
    )(weights, side, new_kv, own_kv, other_values)


def settle(main, stats, n_heads, stat_row, n_target, copies):
    n_src = main.shape[0]
    depth = main.shape[2]
    heads_root = n_heads ** (-0.5)
    heads_out = n_heads // n_target
    n_out = n_target * len(copies(0))

    def body(main_ref, stat_ref, out_ref):
        peaks, totals = [], []
        for b in range(n_src):
            part = stat_ref[b, stat_row : stat_row + STAT_ROWS, :].astype(jnp.float32)
            peaks.append(part[0:1] + part[1:2] + part[2:3])
            totals.append(part[3:4] + part[4:5] + part[5:6])
        peak = functools.reduce(jnp.maximum, peaks)
        scales = [jnp.exp(p - peak) for p in peaks]
        total = functools.reduce(jnp.add, [s * t for s, t in zip(scales, totals)])
        common = lax.broadcasted_iota(jnp.int32, (n_heads, n_heads), 0) & lax.broadcasted_iota(
            jnp.int32, (n_heads, n_heads), 1
        )
        bits = (n_heads - 1).bit_length()
        parity = common
        for bit in range(1, bits):
            parity = parity ^ (common >> bit)
        sign = jnp.where((parity & 1) == 0, heads_root, -heads_root)
        acc = jnp.zeros((n_heads, depth), jnp.float32)
        for b in range(n_src):
            mixed = sign * (scales[b] / total)
            high = mixed.astype(jnp.bfloat16)
            low = (mixed - high.astype(jnp.float32)).astype(jnp.bfloat16)
            value = main_ref[b, 0:n_heads, :]
            acc = acc + jnp.dot(high, value, preferred_element_type=jnp.float32)
            acc = acc + jnp.dot(low, value, preferred_element_type=jnp.float32)
        rotated = acc.astype(jnp.bfloat16)
        for h in range(n_target):
            for spot in copies(h):
                out_ref[spot] = rotated[h * heads_out : (h + 1) * heads_out]

    return pl.pallas_call(
        body,
        out_shape=jax.ShapeDtypeStruct((n_out, heads_out, depth), jnp.bfloat16),
        in_specs=[pl.BlockSpec(memory_space=VMEM)] * 2,
        out_specs=pl.BlockSpec(memory_space=VMEM),
        compiler_params=pltpu.CompilerParams(vmem_limit_bytes=16 * MIB),
        name="settle",
    )(main, stats)


def project(own_share, rows, early, wo, n_block, tiles, spot):
    n_all, heads_here, _ = rows.shape
    n_early, depth, piece = early.shape
    n_late = n_block - n_early
    n_rows = n_all // len(tiles)

    def body(own_ref, x_ref, early_ref, wo_ref, out_ref, late, wide, packed, sem):
        fetch = weight_fetch(wo_ref, late, sem, own_ref[0], n_block, piece)
        fetch_wo = [fetch(n_early + b, b) for b in range(n_late)]
        for copy in fetch_wo:
            copy.start()

        @pl.when(own_ref[0] >= 0)
        def _():
            wide[...] = x_ref[...].astype(jnp.float32).reshape(n_all * heads_here, HD)
            for j in range(heads_here):
                pieces = [
                    wide[pl.ds(first * heads_here + j, n_rows, stride=heads_here * step), :]
                    for first, step in tiles
                ]
                packed[:, HD * j : HD * (j + 1)] = jnp.concatenate(pieces, axis=0).astype(jnp.bfloat16)
            x = packed[...]
            for b in range(n_block):
                if b < n_early:
                    block = early_ref[b]
                else:
                    fetch_wo[b - n_early].wait()
                    block = late[b - n_early]
                share = jnp.dot(x, block, preferred_element_type=jnp.float32)
                for s in range(len(tiles)):
                    out_ref[spot(b, s)] = share[s * n_rows : (s + 1) * n_rows].astype(jnp.bfloat16)

    in_vmem = pl.BlockSpec(memory_space=VMEM)
    return pl.pallas_call(
        body,
        out_shape=jax.ShapeDtypeStruct((n_block * len(tiles), n_rows, piece), jnp.bfloat16),
        in_specs=[
            pl.BlockSpec(memory_space=SMEM), in_vmem, in_vmem, pl.BlockSpec(memory_space=HBM)
        ],
        out_specs=in_vmem,
        scratch_shapes=[
            pltpu.VMEM((n_late, depth, piece), wo.dtype),
            pltpu.VMEM((n_all * heads_here, HD), jnp.float32),
            pltpu.VMEM((n_all, heads_here * HD), jnp.bfloat16),
            pltpu.SemaphoreType.DMA((n_late,)),
        ],
        compiler_params=pltpu.CompilerParams(vmem_limit_bytes=24 * MIB),
        name="project",
    )(own_share, rows, early, in_place(wo))


def finish(shares, scales, residual, n_head, n_share, spot):
    piece = shares.shape[2]

    n_rows = shares.shape[1]

    def body(share_ref, scale_ref, res_ref, out_ref, held):
        for s in range(n_share):
            total = share_ref[spot(0, s)].astype(jnp.float32)
            for h in range(1, n_head):
                total = total + share_ref[spot(h, s)].astype(jnp.float32)
            for c in range(piece // HD):
                held[s * (piece // HD) + c] = total[:, HD * c : HD * (c + 1)]
        for c in range(n_share * piece // HD):
            cols = slice(HD * c, HD * (c + 1))
            ordered = [held[c, pl.ds(p, n_rows // 2, stride=2), :] for p in range(2)]
            total = jnp.concatenate(ordered, axis=0)
            out_ref[:, cols] = (
                res_ref[:, cols].astype(jnp.float32) + total * scale_ref[:, cols]
            ).astype(jnp.bfloat16)

    return pl.pallas_call(
        body,
        out_shape=jax.ShapeDtypeStruct(residual.shape, jnp.bfloat16),
        in_specs=[pl.BlockSpec(memory_space=VMEM)] * 3,
        out_specs=pl.BlockSpec(memory_space=VMEM),
        scratch_shapes=[pltpu.VMEM((n_share * piece // HD, n_rows, HD), jnp.float32)],
        compiler_params=pltpu.CompilerParams(vmem_limit_bytes=16 * MIB),
        name="finish",
    )(shares, scales, residual)


def exchange(block, axes, groups=None):
    return lax.all_to_all(
        block, axes, split_axis=0, concat_axis=0, tiled=True, axis_index_groups=groups
    )


def on_device(
    queries, new_kv, positions, lengths, kv_codes, kv_scales, wo_codes, wo_scales, residual
):
    n_head = lax.axis_size("head")
    n_dp = lax.axis_size("dp")
    my_head = lax.axis_index("head")
    n_rows, width = queries.shape
    heads_here = width // HD
    n_heads = heads_here * n_head
    block_len = kv_codes.shape[2]
    own_cols = wo_codes.shape[1] // n_head
    n_group = lax.axis_size("group")
    if own_cols % (n_group * n_dp * 128):
        n_group = 1
    n_share = n_group * n_dp
    piece = own_cols // n_share
    my_share = lax.axis_index("dp")
    axes = ("head", "dp")
    if n_group > 1:
        my_share = my_share + n_dp * lax.axis_index("group")
        axes = ("group", "head", "dp")

    def spot(head, share):
        return (share // n_dp * n_head + head) * n_dp + share % n_dp

    half = n_rows // 2
    n_line = n_head // 2
    my_line = my_head // 2
    parity = (my_head % 2).astype(jnp.int32)
    pairs = [(i, i ^ 1) for i in range(n_head)]
    lines = [list(range(p, n_head, 2)) for p in range(2)]

    own_half = parity.reshape(1)
    messages, keys_out, values_out, scales_out = prepare(
        own_half, queries, kv_codes, kv_scales, n_head
    )
    other_keys = lax.ppermute(keys_out, "head", pairs)
    other_scales = lax.ppermute(scales_out, "head", pairs)
    gathered = exchange(messages, "head")
    other_values = lax.ppermute(values_out, "head", pairs)
    cosine, sine = rotary_tables(positions)
    own_share = my_share.reshape(1).astype(jnp.int32)
    facts = [parity * half, my_head * block_len, (my_head ^ 1) * block_len, my_line, my_share]
    facts = jnp.concatenate([lengths] + [fact.astype(jnp.int32).reshape(1) for fact in facts])
    new_staged, kv_staged, scales_staged = stage(
        own_half, (new_kv, kv_codes, kv_scales)
    )
    weights, side, early = score(
        facts, gathered, cosine, sine, new_staged, kv_staged, other_keys, scales_staged,
        other_scales, wo_codes, EARLY_EIGHTHS * n_head // 8, piece,
    )
    partial = blend(weights, side, new_staged, kv_staged, other_values)
    own_share, partial = lax.optimization_barrier((own_share, partial))

    cuts = max(1, n_line // half)
    depth = HD // cuts
    if cuts == 1:
        main = exchange(partial, "head", lines)
        stats, stat_row = main, n_heads
    else:
        values = partial[:, :n_heads].reshape(half, n_heads, cuts, depth).swapaxes(1, 2)
        stats = partial[:, n_heads:].reshape(half, 1, STAT_ROWS * cuts, depth)
        stats = jnp.broadcast_to(stats, (half, cuts) + stats.shape[2:])
        message = jnp.concatenate([values, stats], axis=2)
        received = exchange(message.reshape((n_line,) + message.shape[2:]), "head", lines)
        main, stat_row = received[:, :n_heads], 0
        stats = received[:, n_heads:].reshape(n_line, STAT_ROWS, HD)
    copies = settle(
        main, stats, n_heads, stat_row, n_head, lambda h: [spot(h, s) for s in range(n_share)]
    )
    rows = exchange(copies, axes)
    if cuts > 1:
        rows = rows.reshape(n_group, half, cuts, 2, n_dp, heads_here, depth)
        rows = rows.transpose(0, 1, 3, 4, 5, 2, 6).reshape(n_rows * n_share, heads_here, HD)
    tiles = [(s // n_dp * n_rows * n_dp + s % n_dp, n_dp) for s in range(n_share)]
    shares = exchange(project(own_share, rows, early, wo_codes, n_head, tiles, spot), axes)
    return finish(shares, wo_scales.reshape(1, own_cols), residual, n_head, n_share, spot)


def solution(mesh):
    placed = (
        P(("group", "dp"), "head"),
        P(("group", "dp"), None, None),
        P(("group", "dp")),
        P(("group", "dp")),
        P(("group", "dp"), None, "head", None),
        P(("group", "dp"), None, None, "head"),
        P("head", None),
        P("head"),
        P(("group", "dp"), "head"),
    )
    return jax.shard_map(
        on_device, mesh=mesh, in_specs=placed, out_specs=P(("group", "dp"), "head"), check_vma=False
    )
```
